256 devices in a mesh: gx: 16 (over z, core), gy: 16 (over y, x).
Axes of the slice: x: 4, y: 4, z: 8, core: 2. Of those that a mesh axis runs over, the one named last changes fastest.
Arguments:
- fields: float32 [2, 2048, 2048], P(None, 'gy', 'gx'), may hold values from -8 to 8
- material: int32 [2048, 2048], P('gy', 'gx'), may hold values from 0 to 7
- conduct: float32 [2, 8], replicated, may hold values from 0.25 to 4
- joints_x: int32 [2048, 8], P('gy'), may hold values from 1 to 2047
- joints_y: int32 [2048, 8], P('gx'), may hold values from 1 to 2047
Outputs:
- half_step: float32 [2, 2048, 2048], P(None, 'gy', 'gx')
- advanced: float32 [2, 2048, 2048], P(None, 'gy', 'gx')
The draws below stay inside these ranges and needn't reach their ends.
Inputs may be any that keep to these rules, and one draw needn't show every extreme that they name: `joints_x`: entries of one row may repeat. `joints_y`: entries of one column may repeat.
All inputs are finite; a program needn't handle non-finite values.
Results may differ from the reference program's by a relative error of at most 0.0015.
Values sent between devices are 32-bit elements; how exact they have to be, the bound alone decides.
No kernel may reach another device: no remote copies, remote signals or barrier semaphores. Data moves between devices by JAX's collectives and lax.ppermute only.
A program may use at most 64 MiB of HBM per device.

```python
import math
import jax
import jax.numpy as jnp
from jax import lax

JOINTS = 8
MATERIALS = 8
FOURIER = 8192
DRYING = 4096
NX = 2048
NY = 2048


def draw_fields(key, part):
    key_noise, key_region = jax.random.split(key, 2)
    noise_part = jax.random.normal(key_noise, (2, NY, NX), jnp.float32)
    region = jax.random.normal(key_region, (2, 16, 16), jnp.float32) * 2.0
    region = jnp.repeat(jnp.repeat(region, NY // 16, axis=1), NX // 16, axis=2)
    return jnp.clip(noise_part + region, -8.0, 8.0)


def place_ends(result, stream_key, smallest, top_value):
    index_at = [jax.random.randint(jax.random.fold_in(stream_key, axis), (), 0, length) for axis, length in enumerate(result.shape)]
    widest = result.shape.index(max(result.shape))
    next_to = index_at[:widest] + [(index_at[widest] + 1) % result.shape[widest]] + index_at[widest + 1:]
    return result.at[tuple(index_at)].set(smallest).at[tuple(next_to)].set(top_value)


def setup_inputs(seed: int = 0) -> dict:
    streams_of = jax.random.split(jax.random.key(seed), 6)
    return {
        "fields": draw_fields(jax.random.fold_in(streams_of[5], 71), 0),
        "material": place_ends(jax.random.randint(streams_of[1], (NY, NX), 0, MATERIALS), jax.random.fold_in(streams_of[1], 1), 0, MATERIALS - 1).astype(jnp.int32),
        "conduct": jnp.clip(jnp.exp(jax.random.uniform(streams_of[2], (2, MATERIALS), jnp.float32, math.log(0.25), math.log(4.0))), 0.25, 4.0),
        "joints_x": place_ends(jax.random.randint(streams_of[3], (NY, JOINTS), 1, NX), jax.random.fold_in(streams_of[3], 1), 1, NX - 1).astype(jnp.int32),
        "joints_y": place_ends(jax.random.randint(streams_of[4], (NX, JOINTS), 1, NY), jax.random.fold_in(streams_of[4], 1), 1, NY - 1).astype(jnp.int32),
    }


def line_faces(conduction, cut_mask, face_scale):
    interior = face_scale[:, None, None] * 0.5 * (conduction[:, :, :-1] + conduction[:, :, 1:]) * (1.0 - cut_mask[None, :, 1:])
    border = jnp.zeros((conduction.shape[0], conduction.shape[1], 1), jnp.float32)
    return jnp.concatenate([border, interior, border], axis=2)

def line_solve(face_coef, right_side):
    lower = -face_coef[..., :-1]
    upper = -face_coef[..., 1:]
    diagonal = 1.0 + face_coef[..., :-1] + face_coef[..., 1:]
    return lax.linalg.tridiagonal_solve(lower, diagonal, upper, right_side[..., None])[..., 0]

def reference(fields, material, conduct, joints_x, joints_y):
    conduction = conduct[:, material]
    face_scale = jnp.array([FOURIER, DRYING], jnp.float32)
    cut_x = jnp.zeros((NY, NX), jnp.float32).at[jnp.arange(NY, dtype=jnp.int32)[:, None], joints_x].set(1.0)
    cut_y = jnp.zeros((NX, NY), jnp.float32).at[jnp.arange(NX, dtype=jnp.int32)[:, None], joints_y].set(1.0)
    half_step = line_solve(line_faces(conduction, cut_x, face_scale), fields)
    turned = jnp.transpose(conduction, (0, 2, 1))
    advanced = line_solve(line_faces(turned, cut_y, face_scale), jnp.transpose(half_step, (0, 2, 1)))
    return (half_step, jnp.transpose(advanced, (0, 2, 1)))
```

```python
import jax
import jax.numpy as jnp
from jax import lax
from jax.experimental import pallas as pl
from jax.experimental.pallas import tpu as pltpu
from jax.sharding import PartitionSpec as P

MATERIALS = 8
FOURIER = 8192
DRYING = 4096
HALF_SCALE = (FOURIER * 0.5, DRYING * 0.5)

CHUNKS = 8
DEPTH = 16
SIDE = 128
DEVICES = 16
ROWS = 16

G_LOW, G_HIGH, LINK, S_LOW, S_HIGH, C_LOW, C_HIGH, OPEN = range(8)


def sublane():
    return lax.broadcasted_iota(jnp.int32, (CHUNKS, SIDE), 0)


def rolled(x, shift):
    return pltpu.roll(x, shift % CHUNKS, 0)


def conductivities(load, conduct_ref):
    out = ([], [])
    for k in range(DEPTH):
        m = load(k)
        bits = [(m & b) != 0 for b in (1, 2, 4)]
        for c in range(2):
            values = [conduct_ref[c, q] * HALF_SCALE[c] for q in range(MATERIALS)]
            for bit in bits:
                values = [
                    jnp.where(bit, values[i + 1], values[i]) for i in range(0, len(values), 2)
                ]
            out[c].append(values[0])
    return out


def cut_bits(joints_ref, base):
    lane_joints = joints_ref[...] - base
    chunk_start = sublane() * DEPTH
    flags = jnp.zeros((CHUNKS, SIDE), jnp.int32)
    for q in range(joints_ref.shape[0]):
        place = jnp.broadcast_to(lane_joints[q : q + 1, :], (CHUNKS, SIDE)) - chunk_start
        inside = (place >= 0) & (place < DEPTH)
        flags = flags | jnp.where(inside, jnp.left_shift(1, place & (DEPTH - 1)), 0)
    return flags


def face_links(cells, flags):
    links = []
    for k in range(DEPTH):
        before = rolled(cells[DEPTH - 1], 1) if k == 0 else cells[k - 1]
        links.append(jnp.where((flags & (1 << k)) != 0, 0.0, before + cells[k]))
    return links


ORDER = [
    (m, m - half, m + half)
    for half in (1, 2, 4, 8)
    for m in range(half - 1, DEPTH - 1, 2 * half)
]


def factor_chunk(links):
    first = sublane() == 0
    ground = {k: jnp.ones((CHUNKS, SIDE), jnp.float32) for k in range(DEPTH)}
    ground[-1] = jnp.zeros((CHUNKS, SIDE), jnp.float32)
    below = {k: links[k] for k in range(DEPTH)}
    factors = []
    for m, low, high in ORDER:
        a, b, g = below[m], below[high], ground[m]
        inverse = 1.0 / (a + b + g)
        if m == 0:
            inverse = jnp.where(first, 0.0, inverse)
        to_low, to_high = a * inverse, b * inverse
        if m == 0:
            to_low = jnp.where(first, 1.0, to_low)
        ground[low] = ground[low] + to_low * g
        ground[high] = ground[high] + to_high * g
        below[high] = to_low * b
        factors.append((to_low, to_high, inverse))
    return factors, (ground[-1], ground[DEPTH - 1], below[DEPTH - 1])


def source_chunk(factors, sources):
    source = dict(enumerate(sources))
    source[-1] = jnp.zeros((CHUNKS, SIDE), jnp.float32)
    offsets = []
    for (m, low, high), (to_low, to_high, inverse) in zip(ORDER, factors):
        s = source[m]
        source[low] = source[low] + to_low * s
        source[high] = source[high] + to_high * s
        offsets.append(inverse * s)
    return offsets, (source[-1], source[DEPTH - 1])


def join_factor(a, b):
    ground = a[1] + b[0]
    inverse = 1.0 / (a[2] + b[2] + ground)
    to_low, to_high = a[2] * inverse, b[2] * inverse
    joined = (a[0] + to_low * ground, b[1] + to_high * ground, to_low * b[2])
    return (to_low, to_high, inverse), joined


def join_source(factor, a, b):
    to_low, to_high, inverse = factor
    s = a[1] + b[0]
    return inverse * s, (a[0] + to_low * s, b[1] + to_high * s)


def factor_tree(element):
    factors = []
    for step in (1, 2, 4):
        factor, element = join_factor(element, [rolled(x, -step) for x in element])
        factors.append(factor)
    return factors, element


def source_tree(factors, source):
    offsets = []
    for step, factor in zip((1, 2, 4), factors):
        offset, source = join_source(factor, source, [rolled(x, -step) for x in source])
        offsets.append(offset)
    return offsets, source


def solve_tree(factors, offsets, low, high):
    row = sublane()
    for step, (to_low, to_high, _), offset in reversed(list(zip((1, 2, 4), factors, offsets))):
        middle = offset + to_low * low + to_high * high
        upper = (row & step) != 0
        low, high = jnp.where(upper, rolled(middle, step), low), jnp.where(
            upper, rolled(high, step), middle
        )
    return low, high


def solve_chunk(factors, offsets, low, high):
    h = {-1: low, DEPTH - 1: high}
    for (m, lo, hi), (to_low, to_high, _), offset in reversed(list(zip(ORDER, factors, offsets))):
        h[m] = offset + to_low * h[lo] + to_high * h[hi]
    return [h[k] for k in range(DEPTH)]


def outer_ends(gathered_ref, ring_ref, me):
    for d in range(DEVICES):
        ring_ref[d * ROWS : (d + 1) * ROWS, :] = gathered_ref[lax.rem(me + 1 + d, DEVICES)]
    own = sublane() == CHUNKS - 1
    ends = []
    for c in range(2):

        def part(q, odd):
            return ring_ref[pl.ds(odd * ROWS + 8 * c + q, 8, stride=2 * ROWS), :]

        def gate(odd):
            return ring_ref[pl.ds(odd * ROWS + OPEN, 8, stride=2 * ROWS), :]

        elements, sources = [], []
        for odd in range(2):
            before = part(C_HIGH, 0) if odd else rolled(part(C_HIGH, 1), 1)
            entry = (before + part(C_LOW, odd)) * gate(odd)
            zero = jnp.zeros_like(entry)
            factor, element = join_factor(
                (zero, zero, entry), [part(q, odd) for q in (G_LOW, G_HIGH, LINK)]
            )
            _, source = join_source(factor, (zero, zero), [part(q, odd) for q in (S_LOW, S_HIGH)])
            if odd:
                element = [
                    jnp.where(own, y, x) for x, y in zip(element, (zero, zero, entry))
                ]
                source = [jnp.where(own, 0.0, x) for x in source]
            elements.append(element)
            sources.append(source)
        factor, element = join_factor(*elements)
        _, source = join_source(factor, *sources)
        factors, element = factor_tree(element)
        _, source = source_tree(factors, source)

        def mine(q):
            at = (DEVICES - 1) * ROWS + 8 * c + q
            return ring_ref[at : at + 1, :]

        g_low = mine(G_LOW) + element[1][0:1, :]
        g_high = mine(G_HIGH) + element[0][0:1, :]
        link = mine(LINK) + element[2][0:1, :]
        s_low = mine(S_LOW) + source[1][0:1, :]
        s_high = mine(S_HIGH) + source[0][0:1, :]
        inverse = 1.0 / (g_low * g_high + link * (g_low + g_high))
        low = (s_low * (g_high + link) + link * s_high) * inverse
        high = (s_high * (g_low + link) + link * s_low) * inverse
        ends.append(
            (jnp.broadcast_to(low, (CHUNKS, SIDE)), jnp.broadcast_to(high, (CHUNKS, SIDE)))
        )
    return ends


def save(ref, c, at, values):
    for i, x in enumerate(values):
        ref[c, at + i] = x


def load_factors(ref, c, count, at=0):
    return [tuple(ref[c, at + 3 * i + j] for j in range(3)) for i in range(count)]


CELLS = len(ORDER)
STORED = 3 * CELLS + 9
OFFSETS = CELLS + 3


def flatten(factors):
    return [x for factor in factors for x in factor]


def static_rows(pay_ref, c, element, cells, flags, is_first):
    for q, x in zip((G_LOW, G_HIGH, LINK), element):
        pay_ref[8 * c + q : 8 * c + q + 1, :] = x[0:1, :]
    pay_ref[8 * c + C_LOW : 8 * c + C_LOW + 1, :] = cells[0][0:1, :]
    pay_ref[8 * c + C_HIGH : 8 * c + C_HIGH + 1, :] = cells[DEPTH - 1][CHUNKS - 1 : CHUNKS, :]
    shut = ((flags[0:1, :] & 1) != 0) | is_first
    pay_ref[8 * c + OPEN : 8 * c + OPEN + 1, :] = jnp.where(shut, 0.0, 1.0)


def source_rows(pay_ref, c, source):
    for q, x in zip((S_LOW, S_HIGH), source):
        pay_ref[8 * c + q : 8 * c + q + 1, :] = x[0:1, :]


def spread(pay_ref, out_ref):
    pay = pay_ref[...]
    for d in range(DEVICES):
        out_ref[d] = pay


def reduce_kernel(
    fields_ref, material_ref, conduct_ref, joints_x_ref, joints_y_ref,
    out_ref, x_factor_ref, x_offset_ref, y_factor_ref, y_pay_ref,
    turned_ref, kind_ref, pay_ref,
):
    at_x, at_y = lax.axis_index("gx"), lax.axis_index("gy")
    kind_ref[...] = material_ref[...].T
    for c in range(2):
        turned_ref[c] = fields_ref[c].T
    flags = cut_bits(joints_x_ref, at_x * SIDE)
    cells = conductivities(lambda k: kind_ref[pl.ds(k, CHUNKS, stride=DEPTH), :], conduct_ref)
    for c in range(2):
        factors, element = factor_chunk(face_links(cells[c], flags))
        sources = [turned_ref[c, pl.ds(k, CHUNKS, stride=DEPTH), :] for k in range(DEPTH)]
        offsets, source = source_chunk(factors, sources)
        tree, element = factor_tree(element)
        tree_offsets, source = source_tree(tree, source)
        save(x_factor_ref, c, 0, flatten(factors + tree))
        save(x_offset_ref, c, 0, offsets + tree_offsets)
        static_rows(pay_ref, c, element, cells[c], flags, at_x == 0)
        source_rows(pay_ref, c, source)
    spread(pay_ref, out_ref)
    flags = cut_bits(joints_y_ref, at_y * SIDE)
    cells = conductivities(lambda k: material_ref[pl.ds(k, CHUNKS, stride=DEPTH), :], conduct_ref)
    y_pay_ref[...] = jnp.zeros_like(y_pay_ref)
    for c in range(2):
        factors, element = factor_chunk(face_links(cells[c], flags))
        tree, element = factor_tree(element)
        save(y_factor_ref, c, 0, flatten(factors + tree))
        static_rows(y_pay_ref, c, element, cells[c], flags, at_y == 0)


def turn_kernel(
    gathered_ref, x_factor_ref, x_offset_ref, y_factor_ref, y_pay_ref,
    half_ref, out_ref, y_offset_ref,
    ring_ref, turned_ref, pay_ref,
):
    ends = outer_ends(gathered_ref, ring_ref, lax.axis_index("gx"))
    pay_ref[...] = y_pay_ref[...]
    for c in range(2):
        factors = load_factors(x_factor_ref, c, CELLS)
        tree = load_factors(x_factor_ref, c, 3, 3 * CELLS)
        offsets = [x_offset_ref[c, i] for i in range(OFFSETS)]
        low, high = solve_tree(tree, offsets[CELLS:], *ends[c])
        for k, h in enumerate(solve_chunk(factors, offsets[:CELLS], low, high)):
            turned_ref[c, pl.ds(k, CHUNKS, stride=DEPTH), :] = h
        half_ref[c] = turned_ref[c].T
    for c in range(2):
        factors = load_factors(y_factor_ref, c, CELLS)
        tree = load_factors(y_factor_ref, c, 3, 3 * CELLS)
        sources = [half_ref[c, pl.ds(k, CHUNKS, stride=DEPTH), :] for k in range(DEPTH)]
        offsets, source = source_chunk(factors, sources)
        tree_offsets, source = source_tree(tree, source)
        save(y_offset_ref, c, 0, offsets + tree_offsets)
        source_rows(pay_ref, c, source)
    spread(pay_ref, out_ref)


def finish_kernel(gathered_ref, y_factor_ref, y_offset_ref, advanced_ref, ring_ref):
    ends = outer_ends(gathered_ref, ring_ref, lax.axis_index("gy"))
    for c in range(2):
        factors = load_factors(y_factor_ref, c, CELLS)
        tree = load_factors(y_factor_ref, c, 3, 3 * CELLS)
        offsets = [y_offset_ref[c, i] for i in range(OFFSETS)]
        low, high = solve_tree(tree, offsets[CELLS:], *ends[c])
        for k, h in enumerate(solve_chunk(factors, offsets[:CELLS], low, high)):
            advanced_ref[c, pl.ds(k, CHUNKS, stride=DEPTH), :] = h


def f32(*shape):
    return jax.ShapeDtypeStruct(shape, jnp.float32)


VMEM = pl.BlockSpec(memory_space=pltpu.VMEM)
SMEM = pl.BlockSpec(memory_space=pltpu.SMEM)
SPREAD = (DEVICES, ROWS, SIDE)
BLOCK = (2, SIDE, SIDE)
FACTORS = (2, STORED, CHUNKS, SIDE)
OFFSET = (2, OFFSETS, CHUNKS, SIDE)


def per_device(fields, material, conduct, joints_x, joints_y):
    with jax.named_scope("reduce_x"):
        pay, x_factor, x_offset, y_factor, y_pay = pl.pallas_call(
            reduce_kernel,
            out_shape=(f32(*SPREAD), f32(*FACTORS), f32(*OFFSET), f32(*FACTORS), f32(ROWS, SIDE)),
            in_specs=[VMEM, VMEM, SMEM, VMEM, VMEM],
            out_specs=(VMEM,) * 5,
            scratch_shapes=[
                pltpu.VMEM(BLOCK, jnp.float32),
                pltpu.VMEM((SIDE, SIDE), jnp.int32),
                pltpu.VMEM((ROWS, SIDE), jnp.float32),
            ],
        )(fields, material, conduct, joints_x.T, joints_y.T)
    with jax.named_scope("exchange_x"):
        gathered = lax.all_to_all(pay, "gx", 0, 0)
    with jax.named_scope("solve_x_reduce_y"):
        half_step, pay, y_offset = pl.pallas_call(
            turn_kernel,
            out_shape=(f32(*BLOCK), f32(*SPREAD), f32(*OFFSET)),
            in_specs=[VMEM] * 5,
            out_specs=(VMEM,) * 3,
            scratch_shapes=[
                pltpu.VMEM((DEVICES * ROWS, SIDE), jnp.float32),
                pltpu.VMEM(BLOCK, jnp.float32),
                pltpu.VMEM((ROWS, SIDE), jnp.float32),
            ],
        )(gathered, x_factor, x_offset, y_factor, y_pay)
    with jax.named_scope("exchange_y"):
        gathered = lax.all_to_all(pay, "gy", 0, 0)
    with jax.named_scope("solve_y"):
        advanced = pl.pallas_call(
            finish_kernel,
            out_shape=f32(*BLOCK),
            in_specs=[VMEM] * 3,
            out_specs=VMEM,
            scratch_shapes=[pltpu.VMEM((DEVICES * ROWS, SIDE), jnp.float32)],
        )(gathered, y_factor, y_offset)
    return (half_step, advanced)


def solution(mesh):
    return jax.shard_map(
        per_device,
        mesh=mesh,
        in_specs=(P(None, "gy", "gx"), P("gy", "gx"), P(), P("gy", None), P("gx", None)),
        out_specs=(P(None, "gy", "gx"), P(None, "gy", "gx")),
        check_vma=False,
    )
```

```python
import jax
import jax.numpy as jnp
from jax import lax
from jax.experimental import pallas as pl
from jax.experimental.pallas import tpu as pltpu
from jax.sharding import PartitionSpec as P

MATERIALS = 8
FOURIER = 8192
DRYING = 4096
HALF_SCALE = (FOURIER * 0.5, DRYING * 0.5)

CHUNKS = 8
DEPTH = 16
SIDE = 128
DEVICES = 16
ROWS = 16

G_LOW, G_HIGH, LINK, S_LOW, S_HIGH, C_LOW, C_HIGH, OPEN = range(8)


def sublane():
    return lax.broadcasted_iota(jnp.int32, (CHUNKS, SIDE), 0)


def rolled(x, shift):
    return pltpu.roll(x, shift % CHUNKS, 0)


def conductivities(load, conduct_ref):
    out = ([], [])
    for k in range(DEPTH):
        m = load(k)
        bits = [(m & b) != 0 for b in (1, 2, 4)]
        for c in range(2):
            values = [conduct_ref[c, q] * HALF_SCALE[c] for q in range(MATERIALS)]
            for bit in bits:
                values = [
                    jnp.where(bit, values[i + 1], values[i]) for i in range(0, len(values), 2)
                ]
            out[c].append(values[0])
    return out


def cut_bits(joints_ref, base):
    lane_joints = joints_ref[...] - base
    chunk_start = sublane() * DEPTH
    flags = jnp.zeros((CHUNKS, SIDE), jnp.int32)
    for q in range(joints_ref.shape[0]):
        place = jnp.broadcast_to(lane_joints[q : q + 1, :], (CHUNKS, SIDE)) - chunk_start
        inside = (place >= 0) & (place < DEPTH)
        flags = flags | jnp.where(inside, jnp.left_shift(1, place & (DEPTH - 1)), 0)
    return flags


def face_links(cells, flags):
    links = []
    for k in range(DEPTH):
        before = rolled(cells[DEPTH - 1], 1) if k == 0 else cells[k - 1]
        links.append(jnp.where((flags & (1 << k)) != 0, 0.0, before + cells[k]))
    return links


ORDER = [
    (m, m - half, m + half)
    for half in (1, 2, 4, 8)
    for m in range(half - 1, DEPTH - 1, 2 * half)
]


def factor_chunk(links):
    first = sublane() == 0
    ground = {k: jnp.ones((CHUNKS, SIDE), jnp.float32) for k in range(DEPTH)}
    ground[-1] = jnp.zeros((CHUNKS, SIDE), jnp.float32)
    below = {k: links[k] for k in range(DEPTH)}
    factors = []
    for m, low, high in ORDER:
        a, b, g = below[m], below[high], ground[m]
        inverse = 1.0 / (a + b + g)
        if m == 0:
            inverse = jnp.where(first, 0.0, inverse)
        to_low, to_high = a * inverse, b * inverse
        if m == 0:
            to_low = jnp.where(first, 1.0, to_low)
        ground[low] = ground[low] + to_low * g
        ground[high] = ground[high] + to_high * g
        below[high] = to_low * b
        factors.append((to_low, to_high, inverse))
    return factors, (ground[-1], ground[DEPTH - 1], below[DEPTH - 1])


def source_chunk(factors, sources):
    source = dict(enumerate(sources))
    source[-1] = jnp.zeros((CHUNKS, SIDE), jnp.float32)
    offsets = []
    for (m, low, high), (to_low, to_high, inverse) in zip(ORDER, factors):
        s = source[m]
        source[low] = source[low] + to_low * s
        source[high] = source[high] + to_high * s
        offsets.append(inverse * s)
    return offsets, (source[-1], source[DEPTH - 1])


def join_factor(a, b):
    ground = a[1] + b[0]
    inverse = 1.0 / (a[2] + b[2] + ground)
    to_low, to_high = a[2] * inverse, b[2] * inverse
    joined = (a[0] + to_low * ground, b[1] + to_high * ground, to_low * b[2])
    return (to_low, to_high, inverse), joined


def join_source(factor, a, b):
    to_low, to_high, inverse = factor
    s = a[1] + b[0]
    return inverse * s, (a[0] + to_low * s, b[1] + to_high * s)


def factor_tree(element):
    factors = []
    for step in (1, 2, 4):
        factor, element = join_factor(element, [rolled(x, -step) for x in element])
        factors.append(factor)
    return factors, element


def source_tree(factors, source):
    offsets = []
    for step, factor in zip((1, 2, 4), factors):
        offset, source = join_source(factor, source, [rolled(x, -step) for x in source])
        offsets.append(offset)
    return offsets, source


def solve_tree(factors, offsets, low, high):
    row = sublane()
    for step, (to_low, to_high, _), offset in reversed(list(zip((1, 2, 4), factors, offsets))):
        middle = offset + to_low * low + to_high * high
        upper = (row & step) != 0
        low, high = jnp.where(upper, rolled(middle, step), low), jnp.where(
            upper, rolled(high, step), middle
        )
    return low, high


def solve_chunk(factors, offsets, low, high):
    h = {-1: low, DEPTH - 1: high}
    for (m, lo, hi), (to_low, to_high, _), offset in reversed(list(zip(ORDER, factors, offsets))):
        h[m] = offset + to_low * h[lo] + to_high * h[hi]
    return [h[k] for k in range(DEPTH)]


def outer_ends(gathered_ref, ring_ref, me):
    for d in range(DEVICES):
        ring_ref[d * ROWS : (d + 1) * ROWS, :] = gathered_ref[lax.rem(me + 1 + d, DEVICES)]
    own = sublane() == CHUNKS - 1
    ends = []
    for c in range(2):

        def part(q, odd):
            return ring_ref[pl.ds(odd * ROWS + 8 * c + q, 8, stride=2 * ROWS), :]

        def gate(odd):
            return ring_ref[pl.ds(odd * ROWS + OPEN, 8, stride=2 * ROWS), :]

        elements, sources = [], []
        for odd in range(2):
            before = part(C_HIGH, 0) if odd else rolled(part(C_HIGH, 1), 1)
            entry = (before + part(C_LOW, odd)) * gate(odd)
            zero = jnp.zeros_like(entry)
            factor, element = join_factor(
                (zero, zero, entry), [part(q, odd) for q in (G_LOW, G_HIGH, LINK)]
            )
            _, source = join_source(factor, (zero, zero), [part(q, odd) for q in (S_LOW, S_HIGH)])
            if odd:
                element = [
                    jnp.where(own, y, x) for x, y in zip(element, (zero, zero, entry))
                ]
                source = [jnp.where(own, 0.0, x) for x in source]
            elements.append(element)
            sources.append(source)
        factor, element = join_factor(*elements)
        _, source = join_source(factor, *sources)
        factors, element = factor_tree(element)
        _, source = source_tree(factors, source)

        def mine(q):
            at = (DEVICES - 1) * ROWS + 8 * c + q
            return ring_ref[at : at + 1, :]

        g_low = mine(G_LOW) + element[1][0:1, :]
        g_high = mine(G_HIGH) + element[0][0:1, :]
        link = mine(LINK) + element[2][0:1, :]
        s_low = mine(S_LOW) + source[1][0:1, :]
        s_high = mine(S_HIGH) + source[0][0:1, :]
        inverse = 1.0 / (g_low * g_high + link * (g_low + g_high))
        low = (s_low * (g_high + link) + link * s_high) * inverse
        high = (s_high * (g_low + link) + link * s_low) * inverse
        ends.append(
            (jnp.broadcast_to(low, (CHUNKS, SIDE)), jnp.broadcast_to(high, (CHUNKS, SIDE)))
        )
    return ends


def save(ref, c, at, values):
    for i, x in enumerate(values):
        ref[c, at + i] = x


def load_factors(ref, c, count, at=0):
    return [tuple(ref[c, at + 3 * i + j] for j in range(3)) for i in range(count)]


CELLS = len(ORDER)
STORED = 3 * CELLS + 9
OFFSETS = CELLS + 3


def flatten(factors):
    return [x for factor in factors for x in factor]


def static_rows(pay_ref, c, element, cells, flags, is_first):
    for q, x in zip((G_LOW, G_HIGH, LINK), element):
        pay_ref[8 * c + q : 8 * c + q + 1, :] = x[0:1, :]
    pay_ref[8 * c + C_LOW : 8 * c + C_LOW + 1, :] = cells[0][0:1, :]
    pay_ref[8 * c + C_HIGH : 8 * c + C_HIGH + 1, :] = cells[DEPTH - 1][CHUNKS - 1 : CHUNKS, :]
    shut = ((flags[0:1, :] & 1) != 0) | is_first
    pay_ref[8 * c + OPEN : 8 * c + OPEN + 1, :] = jnp.where(shut, 0.0, 1.0)


def source_rows(pay_ref, c, source):
    for q, x in zip((S_LOW, S_HIGH), source):
        pay_ref[8 * c + q : 8 * c + q + 1, :] = x[0:1, :]


def spread(pay_ref, out_ref):
    pay = pay_ref[...]
    for d in range(DEVICES):
        out_ref[d] = pay


def reduce_kernel(
    fields_in, material_in, conduct_in, joints_x_in, joints_y_in,
    out_ref, x_factor_ref, x_offset_ref, y_factor_ref, y_pay_ref,
    fields_ref, material_ref, conduct_ref, joints_x_ref, joints_y_ref,
    turned_ref, kind_ref, pay_ref, sems,
):
    at_x, at_y = lax.axis_index("gx"), lax.axis_index("gy")
    copies = [
        pltpu.make_async_copy(source, target, sems.at[i])
        for i, (source, target) in enumerate(
            (
                (material_in, material_ref),
                (conduct_in, conduct_ref),
                (joints_x_in, joints_x_ref),
                (joints_y_in, joints_y_ref),
                (fields_in, fields_ref),
            )
        )
    ]
    for copy in copies:
        copy.start()
    for copy in copies:
        copy.wait()
    kind_ref[...] = material_ref[...].T
    for c in range(2):
        turned_ref[c] = fields_ref[c].T
    flags = cut_bits(joints_x_ref, at_x * SIDE)
    cells = conductivities(lambda k: kind_ref[pl.ds(k, CHUNKS, stride=DEPTH), :], conduct_ref)
    for c in range(2):
        factors, element = factor_chunk(face_links(cells[c], flags))
        sources = [turned_ref[c, pl.ds(k, CHUNKS, stride=DEPTH), :] for k in range(DEPTH)]
        offsets, source = source_chunk(factors, sources)
        tree, element = factor_tree(element)
        tree_offsets, source = source_tree(tree, source)
        save(x_factor_ref, c, 0, flatten(factors + tree))
        save(x_offset_ref, c, 0, offsets + tree_offsets)
        static_rows(pay_ref, c, element, cells[c], flags, at_x == 0)
        source_rows(pay_ref, c, source)
    spread(pay_ref, out_ref)
    flags = cut_bits(joints_y_ref, at_y * SIDE)
    cells = conductivities(lambda k: material_ref[pl.ds(k, CHUNKS, stride=DEPTH), :], conduct_ref)
    y_pay_ref[...] = jnp.zeros_like(y_pay_ref)
    for c in range(2):
        factors, element = factor_chunk(face_links(cells[c], flags))
        tree, element = factor_tree(element)
        save(y_factor_ref, c, 0, flatten(factors + tree))
        static_rows(y_pay_ref, c, element, cells[c], flags, at_y == 0)


def turn_kernel(
    gathered_ref, x_factor_ref, x_offset_ref, y_factor_ref, y_pay_ref,
    half_ref, out_ref, y_offset_ref,
    ring_ref, turned_ref, pay_ref,
):
    ends = outer_ends(gathered_ref, ring_ref, lax.axis_index("gx"))
    pay_ref[...] = y_pay_ref[...]
    for c in range(2):
        factors = load_factors(x_factor_ref, c, CELLS)
        tree = load_factors(x_factor_ref, c, 3, 3 * CELLS)
        offsets = [x_offset_ref[c, i] for i in range(OFFSETS)]
        low, high = solve_tree(tree, offsets[CELLS:], *ends[c])
        for k, h in enumerate(solve_chunk(factors, offsets[:CELLS], low, high)):
            turned_ref[c, pl.ds(k, CHUNKS, stride=DEPTH), :] = h
        half_ref[c] = turned_ref[c].T
    for c in range(2):
        factors = load_factors(y_factor_ref, c, CELLS)
        tree = load_factors(y_factor_ref, c, 3, 3 * CELLS)
        sources = [half_ref[c, pl.ds(k, CHUNKS, stride=DEPTH), :] for k in range(DEPTH)]
        offsets, source = source_chunk(factors, sources)
        tree_offsets, source = source_tree(tree, source)
        save(y_offset_ref, c, 0, offsets + tree_offsets)
        source_rows(pay_ref, c, source)
    spread(pay_ref, out_ref)


def finish_kernel(
    gathered_ref, y_factor_ref, y_offset_ref, half_ref,
    half_out, advanced_out,
    ring_ref, advanced_ref, sems,
):
    copies = [pltpu.make_async_copy(half_ref, half_out, sems.at[2])]
    copies[0].start()
    ends = outer_ends(gathered_ref, ring_ref, lax.axis_index("gy"))
    for c in range(2):
        factors = load_factors(y_factor_ref, c, CELLS)
        tree = load_factors(y_factor_ref, c, 3, 3 * CELLS)
        offsets = [y_offset_ref[c, i] for i in range(OFFSETS)]
        low, high = solve_tree(tree, offsets[CELLS:], *ends[c])
        for k, h in enumerate(solve_chunk(factors, offsets[:CELLS], low, high)):
            advanced_ref[c, pl.ds(k, CHUNKS, stride=DEPTH), :] = h
        copies.append(pltpu.make_async_copy(advanced_ref.at[c], advanced_out.at[c], sems.at[c]))
        copies[-1].start()
    for copy in copies:
        copy.wait()


def f32(*shape):
    return jax.ShapeDtypeStruct(shape, jnp.float32)


VMEM = pl.BlockSpec(memory_space=pltpu.VMEM)
HBM = pl.BlockSpec(memory_space=pltpu.HBM)
SPREAD = (DEVICES, ROWS, SIDE)
PARAMS = pltpu.CompilerParams(vmem_limit_bytes=8 << 20)
BLOCK = (2, SIDE, SIDE)
FACTORS = (2, STORED, CHUNKS, SIDE)
OFFSET = (2, OFFSETS, CHUNKS, SIDE)


def per_device(fields, material, conduct, joints_x, joints_y):
    inputs = (fields, material, conduct, joints_x.T, joints_y.T)
    with jax.named_scope("reduce_x"):
        pay, x_factor, x_offset, y_factor, y_pay = pl.pallas_call(
            reduce_kernel,
            out_shape=(f32(*SPREAD), f32(*FACTORS), f32(*OFFSET), f32(*FACTORS), f32(ROWS, SIDE)),
            in_specs=[HBM] * 5,
            out_specs=(VMEM,) * 5,
            scratch_shapes=[
                pltpu.VMEM(BLOCK, jnp.float32),
                pltpu.VMEM((SIDE, SIDE), jnp.int32),
                pltpu.SMEM(conduct.shape, jnp.float32),
                pltpu.VMEM(joints_x.shape[::-1], jnp.int32),
                pltpu.VMEM(joints_y.shape[::-1], jnp.int32),
                pltpu.VMEM(BLOCK, jnp.float32),
                pltpu.VMEM((SIDE, SIDE), jnp.int32),
                pltpu.VMEM((ROWS, SIDE), jnp.float32),
                pltpu.SemaphoreType.DMA((5,)),
            ],
            compiler_params=PARAMS,
        )(*(pltpu.with_memory_space_constraint(x, pltpu.HBM) for x in inputs))
    with jax.named_scope("exchange_x"):
        gathered = lax.all_to_all(pay, "gx", 0, 0)
    with jax.named_scope("solve_x_reduce_y"):
        half, pay, y_offset = pl.pallas_call(
            turn_kernel,
            out_shape=(f32(*BLOCK), f32(*SPREAD), f32(*OFFSET)),
            in_specs=[VMEM] * 5,
            out_specs=(VMEM,) * 3,
            scratch_shapes=[
                pltpu.VMEM((DEVICES * ROWS, SIDE), jnp.float32),
                pltpu.VMEM(BLOCK, jnp.float32),
                pltpu.VMEM((ROWS, SIDE), jnp.float32),
            ],
            compiler_params=PARAMS,
        )(gathered, x_factor, x_offset, y_factor, y_pay)
    with jax.named_scope("exchange_y"):
        gathered = lax.all_to_all(pay, "gy", 0, 0)
    with jax.named_scope("solve_y"):
        return pl.pallas_call(
            finish_kernel,
            out_shape=(f32(*BLOCK), f32(*BLOCK)),
            in_specs=[VMEM] * 4,
            out_specs=(HBM, HBM),
            scratch_shapes=[
                pltpu.VMEM((DEVICES * ROWS, SIDE), jnp.float32),
                pltpu.VMEM(BLOCK, jnp.float32),
                pltpu.SemaphoreType.DMA((3,)),
            ],
            compiler_params=PARAMS,
        )(gathered, y_factor, y_offset, half)


def solution(mesh):
    return jax.shard_map(
        per_device,
        mesh=mesh,
        in_specs=(P(None, "gy", "gx"), P("gy", "gx"), P(), P("gy", None), P("gx", None)),
        out_specs=(P(None, "gy", "gx"), P(None, "gy", "gx")),
        check_vma=False,
    )
```

```python
import jax
import jax.numpy as jnp
from jax import lax
from jax.experimental import pallas as pl
from jax.experimental.pallas import tpu as pltpu
from jax.sharding import PartitionSpec as P

MATERIALS = 8
FOURIER = 8192
DRYING = 4096
HALF_SCALE = (FOURIER * 0.5, DRYING * 0.5)

CHUNKS = 8
DEPTH = 16
SIDE = 128
DEVICES = 16
ROWS = 16

G_LOW, G_HIGH, LINK, S_LOW, S_HIGH, C_LOW, C_HIGH, OPEN = range(8)


def sublane():
    return lax.broadcasted_iota(jnp.int32, (CHUNKS, SIDE), 0)


def rolled(x, shift):
    return pltpu.roll(x, shift % CHUNKS, 0)


def conductivities(load, conduct_ref):
    out = ([], [])
    for k in range(DEPTH):
        m = load(k)
        bits = [(m & b) != 0 for b in (1, 2, 4)]
        for c in range(2):
            values = [conduct_ref[c, q] * HALF_SCALE[c] for q in range(MATERIALS)]
            for bit in bits:
                values = [
                    jnp.where(bit, values[i + 1], values[i]) for i in range(0, len(values), 2)
                ]
            out[c].append(values[0])
    return out


def cut_bits(joints_ref, base):
    lane_joints = joints_ref[...] - base
    chunk_start = sublane() * DEPTH
    flags = jnp.zeros((CHUNKS, SIDE), jnp.int32)
    for q in range(joints_ref.shape[0]):
        place = jnp.broadcast_to(lane_joints[q : q + 1, :], (CHUNKS, SIDE)) - chunk_start
        inside = (place >= 0) & (place < DEPTH)
        flags = flags | jnp.where(inside, jnp.left_shift(1, place & (DEPTH - 1)), 0)
    return flags


def face_links(cells, flags):
    links = []
    for k in range(DEPTH):
        before = rolled(cells[DEPTH - 1], 1) if k == 0 else cells[k - 1]
        links.append(jnp.where((flags & (1 << k)) != 0, 0.0, before + cells[k]))
    return links


ORDER = [
    (m, m - half, m + half)
    for half in (1, 2, 4, 8)
    for m in range(half - 1, DEPTH - 1, 2 * half)
]


def factor_chunk(links):
    first = sublane() == 0
    ground = {k: jnp.ones((CHUNKS, SIDE), jnp.float32) for k in range(DEPTH)}
    ground[-1] = jnp.zeros((CHUNKS, SIDE), jnp.float32)
    below = {k: links[k] for k in range(DEPTH)}
    factors = []
    for m, low, high in ORDER:
        a, b, g = below[m], below[high], ground[m]
        inverse = 1.0 / (a + b + g)
        if m == 0:
            inverse = jnp.where(first, 0.0, inverse)
        to_low, to_high = a * inverse, b * inverse
        if m == 0:
            to_low = jnp.where(first, 1.0, to_low)
        ground[low] = ground[low] + to_low * g
        ground[high] = ground[high] + to_high * g
        below[high] = to_low * b
        factors.append((to_low, to_high, inverse))
    return factors, (ground[-1], ground[DEPTH - 1], below[DEPTH - 1])


def source_chunk(factors, sources):
    source = dict(enumerate(sources))
    source[-1] = jnp.zeros((CHUNKS, SIDE), jnp.float32)
    offsets = []
    for (m, low, high), (to_low, to_high, inverse) in zip(ORDER, factors):
        s = source[m]
        source[low] = source[low] + to_low * s
        source[high] = source[high] + to_high * s
        offsets.append(inverse * s)
    return offsets, (source[-1], source[DEPTH - 1])


def join_factor(a, b):
    ground = a[1] + b[0]
    inverse = 1.0 / (a[2] + b[2] + ground)
    to_low, to_high = a[2] * inverse, b[2] * inverse
    joined = (a[0] + to_low * ground, b[1] + to_high * ground, to_low * b[2])
    return (to_low, to_high, inverse), joined


def join_source(factor, a, b):
    to_low, to_high, inverse = factor
    s = a[1] + b[0]
    return inverse * s, (a[0] + to_low * s, b[1] + to_high * s)


def factor_tree(element):
    factors = []
    for step in (1, 2, 4):
        factor, element = join_factor(element, [rolled(x, -step) for x in element])
        factors.append(factor)
    return factors, element


def source_tree(factors, source):
    offsets = []
    for step, factor in zip((1, 2, 4), factors):
        offset, source = join_source(factor, source, [rolled(x, -step) for x in source])
        offsets.append(offset)
    return offsets, source


def solve_tree(factors, offsets, low, high):
    row = sublane()
    for step, (to_low, to_high, _), offset in reversed(list(zip((1, 2, 4), factors, offsets))):
        middle = offset + to_low * low + to_high * high
        upper = (row & step) != 0
        low, high = jnp.where(upper, rolled(middle, step), low), jnp.where(
            upper, rolled(high, step), middle
        )
    return low, high


def solve_chunk(factors, offsets, low, high):
    h = {-1: low, DEPTH - 1: high}
    for (m, lo, hi), (to_low, to_high, _), offset in reversed(list(zip(ORDER, factors, offsets))):
        h[m] = offset + to_low * h[lo] + to_high * h[hi]
    return [h[k] for k in range(DEPTH)]


def outer_ends(gathered_ref, ring_ref, me, turn):
    for d in range(DEVICES):
        ring_ref[d * ROWS : (d + 1) * ROWS, :] = gathered_ref[lax.rem(me + (1 + d - turn) % DEVICES, DEVICES)]
    own = sublane() == CHUNKS - 1
    ends = []
    for c in range(2):

        def part(q, odd):
            return ring_ref[pl.ds(odd * ROWS + 8 * c + q, 8, stride=2 * ROWS), :]

        def gate(odd):
            return ring_ref[pl.ds(odd * ROWS + OPEN, 8, stride=2 * ROWS), :]

        elements, sources = [], []
        for odd in range(2):
            before = part(C_HIGH, 0) if odd else rolled(part(C_HIGH, 1), 1)
            entry = (before + part(C_LOW, odd)) * gate(odd)
            zero = jnp.zeros_like(entry)
            factor, element = join_factor(
                (zero, zero, entry), [part(q, odd) for q in (G_LOW, G_HIGH, LINK)]
            )
            _, source = join_source(factor, (zero, zero), [part(q, odd) for q in (S_LOW, S_HIGH)])
            if odd:
                element = [
                    jnp.where(own, y, x) for x, y in zip(element, (zero, zero, entry))
                ]
                source = [jnp.where(own, 0.0, x) for x in source]
            elements.append(element)
            sources.append(source)
        factor, element = join_factor(*elements)
        _, source = join_source(factor, *sources)
        factors, element = factor_tree(element)
        _, source = source_tree(factors, source)

        def mine(q):
            at = (DEVICES - 1) * ROWS + 8 * c + q
            return ring_ref[at : at + 1, :]

        g_low = mine(G_LOW) + element[1][0:1, :]
        g_high = mine(G_HIGH) + element[0][0:1, :]
        link = mine(LINK) + element[2][0:1, :]
        s_low = mine(S_LOW) + source[1][0:1, :]
        s_high = mine(S_HIGH) + source[0][0:1, :]
        inverse = 1.0 / (g_low * g_high + link * (g_low + g_high))
        low = (s_low * (g_high + link) + link * s_high) * inverse
        high = (s_high * (g_low + link) + link * s_low) * inverse
        ends.append(
            (jnp.broadcast_to(low, (CHUNKS, SIDE)), jnp.broadcast_to(high, (CHUNKS, SIDE)))
        )
    return ends


def save(ref, c, at, values):
    for i, x in enumerate(values):
        ref[c, at + i] = x


def load_factors(ref, c, count, at=0):
    return [tuple(ref[c, at + 3 * i + j] for j in range(3)) for i in range(count)]


CELLS = len(ORDER)
STORED = 3 * CELLS + 9
OFFSETS = CELLS + 3


def flatten(factors):
    return [x for factor in factors for x in factor]


def static_rows(pay_ref, c, element, cells, flags, is_first):
    for q, x in zip((G_LOW, G_HIGH, LINK), element):
        pay_ref[8 * c + q : 8 * c + q + 1, :] = x[0:1, :]
    pay_ref[8 * c + C_LOW : 8 * c + C_LOW + 1, :] = cells[0][0:1, :]
    pay_ref[8 * c + C_HIGH : 8 * c + C_HIGH + 1, :] = cells[DEPTH - 1][CHUNKS - 1 : CHUNKS, :]
    shut = ((flags[0:1, :] & 1) != 0) | is_first
    pay_ref[8 * c + OPEN : 8 * c + OPEN + 1, :] = jnp.where(shut, 0.0, 1.0)


def source_rows(pay_ref, c, source):
    for q, x in zip((S_LOW, S_HIGH), source):
        pay_ref[8 * c + q : 8 * c + q + 1, :] = x[0:1, :]


def spread(pay_ref, out_ref):
    pay = pay_ref[...]
    for d in range(DEVICES):
        out_ref[d] = pay


def reduce_kernel(
    fields_in, material_in, conduct_in, joints_x_in, joints_y_in,
    out_ref, x_factor_ref, x_offset_ref, y_factor_ref, y_pay_ref,
    fields_ref, material_ref, conduct_ref, joints_x_ref, joints_y_ref,
    turned_ref, kind_ref, pay_ref, sems,
):
    at_x, at_y = lax.axis_index("gx"), lax.axis_index("gy")
    copies = [
        pltpu.make_async_copy(source, target, sems.at[i])
        for i, (source, target) in enumerate(
            (
                (material_in, material_ref),
                (conduct_in, conduct_ref),
                (joints_x_in, joints_x_ref),
                (joints_y_in, joints_y_ref),
                (fields_in, fields_ref),
            )
        )
    ]
    for copy in copies:
        copy.start()
    for copy in copies:
        copy.wait()
    kind_ref[...] = material_ref[...].T
    for c in range(2):
        turned_ref[c] = fields_ref[c].T
    flags = cut_bits(joints_x_ref, at_x * SIDE)
    cells = conductivities(lambda k: kind_ref[pl.ds(k, CHUNKS, stride=DEPTH), :], conduct_ref)
    for c in range(2):
        factors, element = factor_chunk(face_links(cells[c], flags))
        sources = [turned_ref[c, pl.ds(k, CHUNKS, stride=DEPTH), :] for k in range(DEPTH)]
        offsets, source = source_chunk(factors, sources)
        tree, element = factor_tree(element)
        tree_offsets, source = source_tree(tree, source)
        save(x_factor_ref, c, 0, flatten(factors + tree))
        save(x_offset_ref, c, 0, offsets + tree_offsets)
        static_rows(pay_ref, c, element, cells[c], flags, at_x == 0)
        source_rows(pay_ref, c, source)
    spread(pay_ref, out_ref)
    flags = cut_bits(joints_y_ref, at_y * SIDE)
    cells = conductivities(lambda k: material_ref[pl.ds(k, CHUNKS, stride=DEPTH), :], conduct_ref)
    y_pay_ref[...] = jnp.zeros_like(y_pay_ref)
    for c in range(2):
        factors, element = factor_chunk(face_links(cells[c], flags))
        tree, element = factor_tree(element)
        save(y_factor_ref, c, 0, flatten(factors + tree))
        static_rows(y_pay_ref, c, element, cells[c], flags, at_y == 0)


def turn_kernel(
    gathered_ref, x_factor_ref, x_offset_ref, y_factor_ref, y_pay_ref,
    half_ref, out_ref, y_offset_ref,
    ring_ref, turned_ref, pay_ref,
):
    ends = outer_ends(gathered_ref, ring_ref, lax.axis_index("gx"), TURN_X)
    pay_ref[...] = y_pay_ref[...]
    for c in range(2):
        factors = load_factors(x_factor_ref, c, CELLS)
        tree = load_factors(x_factor_ref, c, 3, 3 * CELLS)
        offsets = [x_offset_ref[c, i] for i in range(OFFSETS)]
        low, high = solve_tree(tree, offsets[CELLS:], *ends[c])
        for k, h in enumerate(solve_chunk(factors, offsets[:CELLS], low, high)):
            turned_ref[c, pl.ds(k, CHUNKS, stride=DEPTH), :] = h
        half_ref[c] = turned_ref[c].T
    for c in range(2):
        factors = load_factors(y_factor_ref, c, CELLS)
        tree = load_factors(y_factor_ref, c, 3, 3 * CELLS)
        sources = [half_ref[c, pl.ds(k, CHUNKS, stride=DEPTH), :] for k in range(DEPTH)]
        offsets, source = source_chunk(factors, sources)
        tree_offsets, source = source_tree(tree, source)
        save(y_offset_ref, c, 0, offsets + tree_offsets)
        source_rows(pay_ref, c, source)
    spread(pay_ref, out_ref)


def finish_kernel(
    gathered_ref, y_factor_ref, y_offset_ref, half_ref,
    half_out, advanced_out,
    ring_ref, advanced_ref, sems,
):
    copies = [pltpu.make_async_copy(half_ref, half_out, sems.at[2])]
    copies[0].start()
    ends = outer_ends(gathered_ref, ring_ref, lax.axis_index("gy"), TURN_Y)
    for c in range(2):
        factors = load_factors(y_factor_ref, c, CELLS)
        tree = load_factors(y_factor_ref, c, 3, 3 * CELLS)
        offsets = [y_offset_ref[c, i] for i in range(OFFSETS)]
        low, high = solve_tree(tree, offsets[CELLS:], *ends[c])
        for k, h in enumerate(solve_chunk(factors, offsets[:CELLS], low, high)):
            advanced_ref[c, pl.ds(k, CHUNKS, stride=DEPTH), :] = h
        copies.append(pltpu.make_async_copy(advanced_ref.at[c], advanced_out.at[c], sems.at[c]))
        copies[-1].start()
    for copy in copies:
        copy.wait()


TURN_X = 8
TURN_Y = 10


def turned_exchange(x, axis, turn):
    group = [(i + turn) % DEVICES for i in range(DEVICES)]
    return lax.all_to_all(x, axis, 0, 0, axis_index_groups=[group])


def f32(*shape):
    return jax.ShapeDtypeStruct(shape, jnp.float32)


VMEM = pl.BlockSpec(memory_space=pltpu.VMEM)
HBM = pl.BlockSpec(memory_space=pltpu.HBM)
SPREAD = (DEVICES, ROWS, SIDE)
PARAMS = pltpu.CompilerParams(vmem_limit_bytes=8 << 20)
BLOCK = (2, SIDE, SIDE)
FACTORS = (2, STORED, CHUNKS, SIDE)
OFFSET = (2, OFFSETS, CHUNKS, SIDE)


def per_device(fields, material, conduct, joints_x, joints_y):
    inputs = (fields, material, conduct, joints_x.T, joints_y.T)
    with jax.named_scope("reduce_x"):
        pay, x_factor, x_offset, y_factor, y_pay = pl.pallas_call(
            reduce_kernel,
            out_shape=(f32(*SPREAD), f32(*FACTORS), f32(*OFFSET), f32(*FACTORS), f32(ROWS, SIDE)),
            in_specs=[HBM] * 5,
            out_specs=(VMEM,) * 5,
            scratch_shapes=[
                pltpu.VMEM(BLOCK, jnp.float32),
                pltpu.VMEM((SIDE, SIDE), jnp.int32),
                pltpu.SMEM(conduct.shape, jnp.float32),
                pltpu.VMEM(joints_x.shape[::-1], jnp.int32),
                pltpu.VMEM(joints_y.shape[::-1], jnp.int32),
                pltpu.VMEM(BLOCK, jnp.float32),
                pltpu.VMEM((SIDE, SIDE), jnp.int32),
                pltpu.VMEM((ROWS, SIDE), jnp.float32),
                pltpu.SemaphoreType.DMA((5,)),
            ],
            compiler_params=PARAMS,
        )(*(pltpu.with_memory_space_constraint(x, pltpu.HBM) for x in inputs))
    with jax.named_scope("exchange_x"):
        gathered = turned_exchange(pay, "gx", TURN_X)
    with jax.named_scope("solve_x_reduce_y"):
        half, pay, y_offset = pl.pallas_call(
            turn_kernel,
            out_shape=(f32(*BLOCK), f32(*SPREAD), f32(*OFFSET)),
            in_specs=[VMEM] * 5,
            out_specs=(VMEM,) * 3,
            scratch_shapes=[
                pltpu.VMEM((DEVICES * ROWS, SIDE), jnp.float32),
                pltpu.VMEM(BLOCK, jnp.float32),
                pltpu.VMEM((ROWS, SIDE), jnp.float32),
            ],
            compiler_params=PARAMS,
        )(gathered, x_factor, x_offset, y_factor, y_pay)
    with jax.named_scope("exchange_y"):
        gathered = turned_exchange(pay, "gy", TURN_Y)
    with jax.named_scope("solve_y"):
        return pl.pallas_call(
            finish_kernel,
            out_shape=(f32(*BLOCK), f32(*BLOCK)),
            in_specs=[VMEM] * 4,
            out_specs=(HBM, HBM),
            scratch_shapes=[
                pltpu.VMEM((DEVICES * ROWS, SIDE), jnp.float32),
                pltpu.VMEM(BLOCK, jnp.float32),
                pltpu.SemaphoreType.DMA((3,)),
            ],
            compiler_params=PARAMS,
        )(gathered, y_factor, y_offset, half)


def solution(mesh):
    return jax.shard_map(
        per_device,
        mesh=mesh,
        in_specs=(P(None, "gy", "gx"), P("gy", "gx"), P(), P("gy", None), P("gx", None)),
        out_specs=(P(None, "gy", "gx"), P(None, "gy", "gx")),
        check_vma=False,
    )
```

```python
import jax
import jax.numpy as jnp
from jax import lax
from jax.experimental import pallas as pl
from jax.experimental.pallas import tpu as pltpu
from jax.sharding import PartitionSpec as P

MATERIALS = 8
FOURIER = 8192
DRYING = 4096
HALF_SCALE = (FOURIER * 0.5, DRYING * 0.5)

CHUNKS = 8
DEPTH = 16
SIDE = 128
DEVICES = 16
ROWS = 16

G_LOW, G_HIGH, LINK, S_LOW, S_HIGH, C_LOW, C_HIGH, OPEN = range(8)


def sublane():
    return lax.broadcasted_iota(jnp.int32, (CHUNKS, SIDE), 0)


def rolled(x, shift):
    return pltpu.roll(x, shift % CHUNKS, 0)


def conductivities(load, conduct_ref):
    out = ([], [])
    for k in range(DEPTH):
        m = load(k)
        bits = [(m & b) != 0 for b in (1, 2, 4)]
        for c in range(2):
            values = [conduct_ref[c, q] * HALF_SCALE[c] for q in range(MATERIALS)]
            for bit in bits:
                values = [
                    jnp.where(bit, values[i + 1], values[i]) for i in range(0, len(values), 2)
                ]
            out[c].append(values[0])
    return out


def cut_bits(joints_ref, base):
    lane_joints = joints_ref[...] - base
    chunk_start = sublane() * DEPTH
    flags = jnp.zeros((CHUNKS, SIDE), jnp.int32)
    for q in range(joints_ref.shape[0]):
        place = jnp.broadcast_to(lane_joints[q : q + 1, :], (CHUNKS, SIDE)) - chunk_start
        inside = (place >= 0) & (place < DEPTH)
        flags = flags | jnp.where(inside, jnp.left_shift(1, place & (DEPTH - 1)), 0)
    return flags


def face_links(cells, flags):
    links = []
    for k in range(DEPTH):
        before = rolled(cells[DEPTH - 1], 1) if k == 0 else cells[k - 1]
        links.append(jnp.where((flags & (1 << k)) != 0, 0.0, before + cells[k]))
    return links


ORDER = [
    (m, m - half, m + half)
    for half in (1, 2, 4, 8)
    for m in range(half - 1, DEPTH - 1, 2 * half)
]


def factor_chunk(links):
    first = sublane() == 0
    ground = {k: jnp.ones((CHUNKS, SIDE), jnp.float32) for k in range(DEPTH)}
    ground[-1] = jnp.zeros((CHUNKS, SIDE), jnp.float32)
    below = {k: links[k] for k in range(DEPTH)}
    factors = []
    for m, low, high in ORDER:
        a, b, g = below[m], below[high], ground[m]
        inverse = 1.0 / (a + b + g)
        if m == 0:
            inverse = jnp.where(first, 0.0, inverse)
        to_low, to_high = a * inverse, b * inverse
        if m == 0:
            to_low = jnp.where(first, 1.0, to_low)
        ground[low] = ground[low] + to_low * g
        ground[high] = ground[high] + to_high * g
        below[high] = to_low * b
        factors.append((to_low, to_high, inverse))
    return factors, (ground[-1], ground[DEPTH - 1], below[DEPTH - 1])


def source_chunk(factors, sources):
    source = dict(enumerate(sources))
    source[-1] = jnp.zeros((CHUNKS, SIDE), jnp.float32)
    offsets = []
    for (m, low, high), (to_low, to_high, inverse) in zip(ORDER, factors):
        s = source[m]
        source[low] = source[low] + to_low * s
        source[high] = source[high] + to_high * s
        offsets.append(inverse * s)
    return offsets, (source[-1], source[DEPTH - 1])


def join_factor(a, b):
    ground = a[1] + b[0]
    inverse = 1.0 / (a[2] + b[2] + ground)
    to_low, to_high = a[2] * inverse, b[2] * inverse
    joined = (a[0] + to_low * ground, b[1] + to_high * ground, to_low * b[2])
    return (to_low, to_high, inverse), joined


def join_source(factor, a, b):
    to_low, to_high, inverse = factor
    s = a[1] + b[0]
    return inverse * s, (a[0] + to_low * s, b[1] + to_high * s)


def factor_tree(element):
    factors = []
    for step in (1, 2, 4):
        factor, element = join_factor(element, [rolled(x, -step) for x in element])
        factors.append(factor)
    return factors, element


def source_tree(factors, source):
    offsets = []
    for step, factor in zip((1, 2, 4), factors):
        offset, source = join_source(factor, source, [rolled(x, -step) for x in source])
        offsets.append(offset)
    return offsets, source


def solve_tree(factors, offsets, low, high):
    row = sublane()
    for step, (to_low, to_high, _), offset in reversed(list(zip((1, 2, 4), factors, offsets))):
        middle = offset + to_low * low + to_high * high
        upper = (row & step) != 0
        low, high = jnp.where(upper, rolled(middle, step), low), jnp.where(
            upper, rolled(high, step), middle
        )
    return low, high


def solve_chunk(factors, offsets, low, high):
    h = {-1: low, DEPTH - 1: high}
    for (m, lo, hi), (to_low, to_high, _), offset in reversed(list(zip(ORDER, factors, offsets))):
        h[m] = offset + to_low * h[lo] + to_high * h[hi]
    return [h[k] for k in range(DEPTH)]


def outer_ends(gathered_ref, ring_ref, me, turn):
    for d in range(DEVICES):
        ring_ref[d * ROWS : (d + 1) * ROWS, :] = gathered_ref[lax.rem(me + (1 + d - turn) % DEVICES, DEVICES)]
    own = sublane() == CHUNKS - 1
    ends = []
    for c in range(2):

        def part(q, odd):
            return ring_ref[pl.ds(odd * ROWS + 8 * c + q, 8, stride=2 * ROWS), :]

        def gate(odd):
            return ring_ref[pl.ds(odd * ROWS + OPEN, 8, stride=2 * ROWS), :]

        elements, sources = [], []
        for odd in range(2):
            before = part(C_HIGH, 0) if odd else rolled(part(C_HIGH, 1), 1)
            entry = (before + part(C_LOW, odd)) * gate(odd)
            zero = jnp.zeros_like(entry)
            factor, element = join_factor(
                (zero, zero, entry), [part(q, odd) for q in (G_LOW, G_HIGH, LINK)]
            )
            _, source = join_source(factor, (zero, zero), [part(q, odd) for q in (S_LOW, S_HIGH)])
            if odd:
                element = [
                    jnp.where(own, y, x) for x, y in zip(element, (zero, zero, entry))
                ]
                source = [jnp.where(own, 0.0, x) for x in source]
            elements.append(element)
            sources.append(source)
        factor, element = join_factor(*elements)
        _, source = join_source(factor, *sources)
        factors, element = factor_tree(element)
        _, source = source_tree(factors, source)

        def mine(q):
            at = (DEVICES - 1) * ROWS + 8 * c + q
            return ring_ref[at : at + 1, :]

        g_low = mine(G_LOW) + element[1][0:1, :]
        g_high = mine(G_HIGH) + element[0][0:1, :]
        link = mine(LINK) + element[2][0:1, :]
        s_low = mine(S_LOW) + source[1][0:1, :]
        s_high = mine(S_HIGH) + source[0][0:1, :]
        inverse = 1.0 / (g_low * g_high + link * (g_low + g_high))
        low = (s_low * (g_high + link) + link * s_high) * inverse
        high = (s_high * (g_low + link) + link * s_low) * inverse
        ends.append(
            (jnp.broadcast_to(low, (CHUNKS, SIDE)), jnp.broadcast_to(high, (CHUNKS, SIDE)))
        )
    return ends


def save(ref, c, at, values):
    for i, x in enumerate(values):
        ref[c, at + i] = x


def load_factors(ref, c, count, at=0):
    return [tuple(ref[c, at + 3 * i + j] for j in range(3)) for i in range(count)]


CELLS = len(ORDER)
STORED = 3 * CELLS + 9
OFFSETS = CELLS + 3


def flatten(factors):
    return [x for factor in factors for x in factor]


def static_rows(pay_ref, c, element, cells, flags, is_first):
    for q, x in zip((G_LOW, G_HIGH, LINK), element):
        pay_ref[8 * c + q : 8 * c + q + 1, :] = x[0:1, :]
    pay_ref[8 * c + C_LOW : 8 * c + C_LOW + 1, :] = cells[0][0:1, :]
    pay_ref[8 * c + C_HIGH : 8 * c + C_HIGH + 1, :] = cells[DEPTH - 1][CHUNKS - 1 : CHUNKS, :]
    shut = ((flags[0:1, :] & 1) != 0) | is_first
    pay_ref[8 * c + OPEN : 8 * c + OPEN + 1, :] = jnp.where(shut, 0.0, 1.0)


def source_rows(pay_ref, c, source):
    for q, x in zip((S_LOW, S_HIGH), source):
        pay_ref[8 * c + q : 8 * c + q + 1, :] = x[0:1, :]


def spread(pay_ref, out_ref):
    pay = pay_ref[...]
    for d in range(DEVICES):
        out_ref[d] = pay


def reduce_kernel(
    fields_in, material_in, conduct_in, joints_x_in, joints_y_in,
    out_ref, x_factor_ref, x_offset_ref, y_factor_ref, y_pay_ref,
    fields_ref, material_ref, conduct_ref, joints_x_ref, joints_y_ref,
    turned_ref, kind_ref, pay_ref, sems,
):
    at_x, at_y = lax.axis_index("gx"), lax.axis_index("gy")
    copies = [
        pltpu.make_async_copy(source, target, sems.at[i])
        for i, (source, target) in enumerate(
            (
                (material_in, material_ref),
                (conduct_in, conduct_ref),
                (joints_x_in, joints_x_ref),
                (joints_y_in, joints_y_ref),
                (fields_in, fields_ref),
            )
        )
    ]
    for copy in copies:
        copy.start()
    for copy in copies:
        copy.wait()
    kind_ref[...] = material_ref[...].T
    for c in range(2):
        turned_ref[c] = fields_ref[c].T
    flags = cut_bits(joints_x_ref, at_x * SIDE)
    cells = conductivities(lambda k: kind_ref[pl.ds(k, CHUNKS, stride=DEPTH), :], conduct_ref)
    for c in range(2):
        factors, element = factor_chunk(face_links(cells[c], flags))
        sources = [turned_ref[c, pl.ds(k, CHUNKS, stride=DEPTH), :] for k in range(DEPTH)]
        offsets, source = source_chunk(factors, sources)
        tree, element = factor_tree(element)
        tree_offsets, source = source_tree(tree, source)
        save(x_factor_ref, c, 0, flatten(factors + tree))
        save(x_offset_ref, c, 0, offsets + tree_offsets)
        static_rows(pay_ref, c, element, cells[c], flags, at_x == 0)
        source_rows(pay_ref, c, source)
    spread(pay_ref, out_ref)
    flags = cut_bits(joints_y_ref, at_y * SIDE)
    cells = conductivities(lambda k: material_ref[pl.ds(k, CHUNKS, stride=DEPTH), :], conduct_ref)
    y_pay_ref[...] = jnp.zeros_like(y_pay_ref)
    for c in range(2):
        factors, element = factor_chunk(face_links(cells[c], flags))
        tree, element = factor_tree(element)
        save(y_factor_ref, c, 0, flatten(factors + tree))
        static_rows(y_pay_ref, c, element, cells[c], flags, at_y == 0)


def turn_kernel(
    gathered_ref, x_factor_ref, x_offset_ref, y_factor_ref, y_pay_ref,
    half_ref, out_ref, y_offset_ref,
    ring_ref, turned_ref, pay_ref,
):
    ends = outer_ends(gathered_ref, ring_ref, lax.axis_index("gx"), TURN_X)
    pay_ref[...] = y_pay_ref[...]
    for c in range(2):
        factors = load_factors(x_factor_ref, c, CELLS)
        tree = load_factors(x_factor_ref, c, 3, 3 * CELLS)
        offsets = [x_offset_ref[c, i] for i in range(OFFSETS)]
        low, high = solve_tree(tree, offsets[CELLS:], *ends[c])
        for k, h in enumerate(solve_chunk(factors, offsets[:CELLS], low, high)):
            turned_ref[c, pl.ds(k, CHUNKS, stride=DEPTH), :] = h
        half_ref[c] = turned_ref[c].T
    for c in range(2):
        factors = load_factors(y_factor_ref, c, CELLS)
        tree = load_factors(y_factor_ref, c, 3, 3 * CELLS)
        sources = [half_ref[c, pl.ds(k, CHUNKS, stride=DEPTH), :] for k in range(DEPTH)]
        offsets, source = source_chunk(factors, sources)
        tree_offsets, source = source_tree(tree, source)
        save(y_offset_ref, c, 0, offsets + tree_offsets)
        source_rows(pay_ref, c, source)
    spread(pay_ref, out_ref)


def finish_kernel(
    gathered_ref, y_factor_ref, y_offset_ref, half_ref,
    half_out, advanced_out,
    ring_ref, advanced_ref, sems,
):
    copies = [pltpu.make_async_copy(half_ref, half_out, sems.at[2])]
    copies[0].start()
    ends = outer_ends(gathered_ref, ring_ref, lax.axis_index("gy"), TURN_Y)
    for c in range(2):
        factors = load_factors(y_factor_ref, c, CELLS)
        tree = load_factors(y_factor_ref, c, 3, 3 * CELLS)
        offsets = [y_offset_ref[c, i] for i in range(OFFSETS)]
        low, high = solve_tree(tree, offsets[CELLS:], *ends[c])
        for k, h in enumerate(solve_chunk(factors, offsets[:CELLS], low, high)):
            advanced_ref[c, pl.ds(k, CHUNKS, stride=DEPTH), :] = h
        copies.append(pltpu.make_async_copy(advanced_ref.at[c], advanced_out.at[c], sems.at[c]))
        copies[-1].start()
    for copy in copies:
        copy.wait()


TURN_X = 11
TURN_Y = 10


def turned_exchange(x, axis, turn):
    group = [(i + turn) % DEVICES for i in range(DEVICES)]
    return lax.all_to_all(x, axis, 0, 0, axis_index_groups=[group])


def f32(*shape):
    return jax.ShapeDtypeStruct(shape, jnp.float32)


VMEM = pl.BlockSpec(memory_space=pltpu.VMEM)
HBM = pl.BlockSpec(memory_space=pltpu.HBM)
SPREAD = (DEVICES, ROWS, SIDE)
PARAMS = pltpu.CompilerParams(vmem_limit_bytes=8 << 20)
BLOCK = (2, SIDE, SIDE)
FACTORS = (2, STORED, CHUNKS, SIDE)
OFFSET = (2, OFFSETS, CHUNKS, SIDE)


def per_device(fields, material, conduct, joints_x, joints_y):
    inputs = (fields, material, conduct, joints_x.T, joints_y.T)
    with jax.named_scope("reduce_x"):
        pay, x_factor, x_offset, y_factor, y_pay = pl.pallas_call(
            reduce_kernel,
            out_shape=(f32(*SPREAD), f32(*FACTORS), f32(*OFFSET), f32(*FACTORS), f32(ROWS, SIDE)),
            in_specs=[HBM] * 5,
            out_specs=(VMEM,) * 5,
            scratch_shapes=[
                pltpu.VMEM(BLOCK, jnp.float32),
                pltpu.VMEM((SIDE, SIDE), jnp.int32),
                pltpu.SMEM(conduct.shape, jnp.float32),
                pltpu.VMEM(joints_x.shape[::-1], jnp.int32),
                pltpu.VMEM(joints_y.shape[::-1], jnp.int32),
                pltpu.VMEM(BLOCK, jnp.float32),
                pltpu.VMEM((SIDE, SIDE), jnp.int32),
                pltpu.VMEM((ROWS, SIDE), jnp.float32),
                pltpu.SemaphoreType.DMA((5,)),
            ],
            compiler_params=PARAMS,
        )(*(pltpu.with_memory_space_constraint(x, pltpu.HBM) for x in inputs))
    with jax.named_scope("exchange_x"):
        gathered = turned_exchange(pay, "gx", TURN_X)
    with jax.named_scope("solve_x_reduce_y"):
        half, pay, y_offset = pl.pallas_call(
            turn_kernel,
            out_shape=(f32(*BLOCK), f32(*SPREAD), f32(*OFFSET)),
            in_specs=[VMEM] * 5,
            out_specs=(VMEM,) * 3,
            scratch_shapes=[
                pltpu.VMEM((DEVICES * ROWS, SIDE), jnp.float32),
                pltpu.VMEM(BLOCK, jnp.float32),
                pltpu.VMEM((ROWS, SIDE), jnp.float32),
            ],
            compiler_params=PARAMS,
        )(gathered, x_factor, x_offset, y_factor, y_pay)
    with jax.named_scope("exchange_y"):
        gathered = turned_exchange(pay, "gy", TURN_Y)
    with jax.named_scope("solve_y"):
        return pl.pallas_call(
            finish_kernel,
            out_shape=(f32(*BLOCK), f32(*BLOCK)),
            in_specs=[VMEM] * 4,
            out_specs=(HBM, HBM),
            scratch_shapes=[
                pltpu.VMEM((DEVICES * ROWS, SIDE), jnp.float32),
                pltpu.VMEM(BLOCK, jnp.float32),
                pltpu.SemaphoreType.DMA((3,)),
            ],
            compiler_params=PARAMS,
        )(gathered, y_factor, y_offset, half)


def solution(mesh):
    return jax.shard_map(
        per_device,
        mesh=mesh,
        in_specs=(P(None, "gy", "gx"), P("gy", "gx"), P(), P("gy", None), P("gx", None)),
        out_specs=(P(None, "gy", "gx"), P(None, "gy", "gx")),
        check_vma=False,
    )
```

```python
import jax
import jax.numpy as jnp
from jax import lax
from jax.experimental import pallas as pl
from jax.experimental.pallas import tpu as pltpu
from jax.sharding import PartitionSpec as P

MATERIALS = 8
FOURIER = 8192
DRYING = 4096
HALF_SCALE = (FOURIER * 0.5, DRYING * 0.5)

CHUNKS = 8
DEPTH = 16
SIDE = 128
DEVICES = 16
ROWS = 16
SLABS, SLAB = 3, 4
G_LOW, G_HIGH, LINK, S_LOW, S_HIGH = range(5)
KIND_LOW, KIND_HIGH, OPEN = 10, 11, 12


def sublane():
    return lax.broadcasted_iota(jnp.int32, (CHUNKS, SIDE), 0)


def rolled(x, shift):
    return pltpu.roll(x, shift % CHUNKS, 0)


def chosen(kind, values):
    for b in (1, 2, 4):
        bit = (kind & b) != 0
        values = [jnp.where(bit, values[i + 1], values[i]) for i in range(0, len(values), 2)]
    return values[0]


def conductivities(load, conduct_ref):
    kinds = [load(k) for k in range(DEPTH)]
    return [
        [
            chosen(kind, [conduct_ref[c, q] * HALF_SCALE[c] for q in range(MATERIALS)])
            for kind in kinds
        ]
        for c in range(2)
    ]


def cut_bits(joints_ref, base):
    lane_joints = joints_ref[...] - base
    chunk_start = sublane() * DEPTH
    flags = jnp.zeros((CHUNKS, SIDE), jnp.int32)
    for q in range(joints_ref.shape[0]):
        place = jnp.broadcast_to(lane_joints[q : q + 1, :], (CHUNKS, SIDE)) - chunk_start
        inside = (place >= 0) & (place < DEPTH)
        flags = flags | jnp.where(inside, jnp.left_shift(1, place & (DEPTH - 1)), 0)
    return flags


def face_links(cells, flags):
    links = []
    for k in range(DEPTH):
        before = rolled(cells[DEPTH - 1], 1) if k == 0 else cells[k - 1]
        links.append(jnp.where((flags & (1 << k)) != 0, 0.0, before + cells[k]))
    return links


ORDER = [
    (m, m - half, m + half)
    for half in (1, 2, 4, 8)
    for m in range(half - 1, DEPTH - 1, 2 * half)
]


def factor_chunk(links):
    first = sublane() == 0
    ground = {k: jnp.ones((CHUNKS, SIDE), jnp.float32) for k in range(DEPTH)}
    ground[-1] = jnp.zeros((CHUNKS, SIDE), jnp.float32)
    below = {k: links[k] for k in range(DEPTH)}
    factors = []
    for m, low, high in ORDER:
        a, b, g = below[m], below[high], ground[m]
        inverse = 1.0 / (a + b + g)
        if m == 0:
            inverse = jnp.where(first, 0.0, inverse)
        to_low, to_high = a * inverse, b * inverse
        if m == 0:
            to_low = jnp.where(first, 1.0, to_low)
        ground[low] = ground[low] + to_low * g
        ground[high] = ground[high] + to_high * g
        below[high] = to_low * b
        factors.append((to_low, to_high, inverse))
    return factors, (ground[-1], ground[DEPTH - 1], below[DEPTH - 1])


def source_chunk(factors, sources):
    source = dict(enumerate(sources))
    source[-1] = jnp.zeros((CHUNKS, SIDE), jnp.float32)
    offsets = []
    for (m, low, high), (to_low, to_high, inverse) in zip(ORDER, factors):
        s = source[m]
        source[low] = source[low] + to_low * s
        source[high] = source[high] + to_high * s
        offsets.append(inverse * s)
    return offsets, (source[-1], source[DEPTH - 1])


def join_factor(a, b):
    ground = a[1] + b[0]
    inverse = 1.0 / (a[2] + b[2] + ground)
    to_low, to_high = a[2] * inverse, b[2] * inverse
    joined = (a[0] + to_low * ground, b[1] + to_high * ground, to_low * b[2])
    return (to_low, to_high, inverse), joined


def join_source(factor, a, b):
    to_low, to_high, inverse = factor
    s = a[1] + b[0]
    return inverse * s, (a[0] + to_low * s, b[1] + to_high * s)


def factor_tree(element):
    factors = []
    for step in (1, 2, 4):
        factor, element = join_factor(element, [rolled(x, -step) for x in element])
        factors.append(factor)
    return factors, element


def source_tree(factors, source):
    offsets = []
    for step, factor in zip((1, 2, 4), factors):
        offset, source = join_source(factor, source, [rolled(x, -step) for x in source])
        offsets.append(offset)
    return offsets, source


def solve_tree(factors, offsets, low, high):
    row = sublane()
    for step, (to_low, to_high, _), offset in reversed(list(zip((1, 2, 4), factors, offsets))):
        middle = offset + to_low * low + to_high * high
        upper = (row & step) != 0
        low, high = jnp.where(upper, rolled(middle, step), low), jnp.where(
            upper, rolled(high, step), middle
        )
    return low, high


def solve_chunk(factors, offsets, low, high):
    h = {-1: low, DEPTH - 1: high}
    for (m, lo, hi), (to_low, to_high, _), offset in reversed(list(zip(ORDER, factors, offsets))):
        h[m] = offset + to_low * h[lo] + to_high * h[hi]
    return [h[k] for k in range(DEPTH)]


def gates(joints_ref):
    joints = joints_ref[...]
    flags = jnp.ones((1, SIDE), jnp.int32)
    for q in range(joints_ref.shape[0]):
        joint = joints[q : q + 1, :]
        at_edge = (joint & (SIDE - 1)) == 0
        device = lax.shift_right_logical(joint, SIDE.bit_length() - 1) & (DEVICES - 1)
        flags = flags | jnp.where(at_edge, jnp.left_shift(1, device), 0)
    row = lax.broadcasted_iota(jnp.int32, (DEVICES, SIDE), 0)
    flags = jnp.broadcast_to(flags, (DEVICES, SIDE))
    return jnp.where((lax.shift_right_logical(flags, row) & 1) != 0, 0.0, 1.0)


def outer_ends(gathered_ref, gates_ref, table_ref, ring_ref, me, turn):
    for d in range(DEVICES):
        member = lax.rem(me + (1 + d - turn) % DEVICES, DEVICES)
        for p in range(SLABS):
            at = d * ROWS + p * SLAB
            ring_ref[at : at + SLAB, :] = gathered_ref[SLABS * member + p]
        device = lax.rem(me + 1 + d, DEVICES)
        ring_ref[d * ROWS + OPEN : d * ROWS + OPEN + 1, :] = gates_ref[pl.ds(device, 1), :]
    own = sublane() == CHUNKS - 1

    def part(row, odd):
        return ring_ref[pl.ds(odd * ROWS + row, 8, stride=2 * ROWS), :]

    kinds_low, kinds_high = (
        [part(row, odd).astype(jnp.int32) for odd in range(2)] for row in (KIND_LOW, KIND_HIGH)
    )
    ends = []
    for c in range(2):
        values = [
            jnp.broadcast_to(table_ref[MATERIALS * c + q : MATERIALS * c + q + 1, :], own.shape)
            for q in range(MATERIALS)
        ]
        cells_low, cells_high = (
            [chosen(kind, values) for kind in kinds] for kinds in (kinds_low, kinds_high)
        )
        elements, sources = [], []
        for odd in range(2):
            before = cells_high[0] if odd else rolled(cells_high[1], 1)
            entry = (before + cells_low[odd]) * part(OPEN, odd)
            zero = jnp.zeros_like(entry)
            factor, element = join_factor(
                (zero, zero, entry), [part(2 * q + c, odd) for q in (G_LOW, G_HIGH, LINK)]
            )
            _, source = join_source(
                factor, (zero, zero), [part(2 * q + c, odd) for q in (S_LOW, S_HIGH)]
            )
            if odd:
                element = [
                    jnp.where(own, y, x) for x, y in zip(element, (zero, zero, entry))
                ]
                source = [jnp.where(own, 0.0, x) for x in source]
            elements.append(element)
            sources.append(source)
        factor, element = join_factor(*elements)
        _, source = join_source(factor, *sources)
        factors, element = factor_tree(element)
        _, source = source_tree(factors, source)

        def mine(q):
            at = (DEVICES - 1) * ROWS + 2 * q + c
            return ring_ref[at : at + 1, :]

        g_low = mine(G_LOW) + element[1][0:1, :]
        g_high = mine(G_HIGH) + element[0][0:1, :]
        link = mine(LINK) + element[2][0:1, :]
        s_low = mine(S_LOW) + source[1][0:1, :]
        s_high = mine(S_HIGH) + source[0][0:1, :]
        inverse = 1.0 / (g_low * g_high + link * (g_low + g_high))
        low = (s_low * (g_high + link) + link * s_high) * inverse
        high = (s_high * (g_low + link) + link * s_low) * inverse
        ends.append(
            (jnp.broadcast_to(low, (CHUNKS, SIDE)), jnp.broadcast_to(high, (CHUNKS, SIDE)))
        )
    return ends


def save(ref, c, at, values):
    for i, x in enumerate(values):
        ref[c, at + i] = x


def load_factors(ref, c, count, at=0):
    return [tuple(ref[c, at + 3 * i + j] for j in range(3)) for i in range(count)]


CELLS = len(ORDER)
STORED = 3 * CELLS + 9
OFFSETS = CELLS + 3


def flatten(factors):
    return [x for factor in factors for x in factor]


def put(pay_ref, row, x):
    pay_ref[row : row + 1, :] = x


def static_rows(pay_ref, c, element):
    for q, x in zip((G_LOW, G_HIGH, LINK), element):
        put(pay_ref, 2 * q + c, x[0:1, :])


def kind_rows(pay_ref, kind_ref):
    for row, at in ((KIND_LOW, 0), (KIND_HIGH, SIDE - 1)):
        put(pay_ref, row, kind_ref[at : at + 1, :].astype(jnp.float32))


def source_rows(pay_ref, c, source):
    for q, x in zip((S_LOW, S_HIGH), source):
        put(pay_ref, 2 * q + c, x[0:1, :])


def spread(pay_ref, out_ref):
    for p in range(SLABS):
        slab = pay_ref[p * SLAB : (p + 1) * SLAB, :]
        for d in range(DEVICES):
            out_ref[SLABS * d + p] = slab


def reduce_kernel(
    fields_in, material_in, conduct_in, joints_x_in, joints_y_in,
    out_ref, x_factor_ref, x_offset_ref, y_factor_ref, y_pay_ref,
    x_gates_ref, y_gates_ref, table_ref,
    fields_ref, material_ref, conduct_ref, joints_x_ref, joints_y_ref,
    turned_ref, kind_ref, pay_ref, sems,
):
    at_x, at_y = lax.axis_index("gx"), lax.axis_index("gy")
    copies = [
        pltpu.make_async_copy(source, target, sems.at[i])
        for i, (source, target) in enumerate(
            (
                (material_in, material_ref),
                (conduct_in, conduct_ref),
                (joints_x_in, joints_x_ref),
                (joints_y_in, joints_y_ref),
                (fields_in.at[0], fields_ref.at[0]),
                (fields_in.at[1], fields_ref.at[1]),
            )
        )
    ]
    for copy in copies:
        copy.start()
    for copy in copies[:4]:
        copy.wait()
    kind_ref[...] = material_ref[...].T
    flags = cut_bits(joints_x_ref, at_x * SIDE)
    cells = conductivities(lambda k: kind_ref[pl.ds(k, CHUNKS, stride=DEPTH), :], conduct_ref)
    chunks = [factor_chunk(face_links(cells[c], flags)) for c in range(2)]
    trees = [factor_tree(element) for _, element in chunks]
    kind_rows(pay_ref, kind_ref)
    for c in range(2):
        static_rows(pay_ref, c, trees[c][1])
        save(x_factor_ref, c, 0, flatten(chunks[c][0] + trees[c][0]))
        copies[4 + c].wait()
        turned_ref[c] = fields_ref[c].T
        sources = [turned_ref[c, pl.ds(k, CHUNKS, stride=DEPTH), :] for k in range(DEPTH)]
        offsets, source = source_chunk(chunks[c][0], sources)
        tree_offsets, source = source_tree(trees[c][0], source)
        save(x_offset_ref, c, 0, offsets + tree_offsets)
        source_rows(pay_ref, c, source)
    spread(pay_ref, out_ref)
    x_gates_ref[...] = gates(joints_x_ref)
    y_gates_ref[...] = gates(joints_y_ref)
    for c in range(2):
        for q in range(MATERIALS):
            table_ref[MATERIALS * c + q : MATERIALS * c + q + 1, :] = jnp.full(
                (1, SIDE), conduct_ref[c, q] * HALF_SCALE[c], jnp.float32
            )
    flags = cut_bits(joints_y_ref, at_y * SIDE)
    cells = conductivities(lambda k: material_ref[pl.ds(k, CHUNKS, stride=DEPTH), :], conduct_ref)
    y_pay_ref[...] = jnp.zeros_like(y_pay_ref)
    kind_rows(y_pay_ref, material_ref)
    for c in range(2):
        factors, element = factor_chunk(face_links(cells[c], flags))
        tree, element = factor_tree(element)
        save(y_factor_ref, c, 0, flatten(factors + tree))
        static_rows(y_pay_ref, c, element)


def turn_kernel(
    gathered_ref, gates_ref, table_ref, x_factor_ref, x_offset_ref, y_factor_ref, y_pay_ref,
    half_ref, out_ref, y_offset_ref,
    ring_ref, turned_ref, pay_ref,
):
    ends = outer_ends(
        gathered_ref, gates_ref, table_ref, ring_ref, lax.axis_index("gx"), TURN_X
    )
    pay_ref[...] = y_pay_ref[...]
    for c in range(2):
        factors = load_factors(x_factor_ref, c, CELLS)
        tree = load_factors(x_factor_ref, c, 3, 3 * CELLS)
        offsets = [x_offset_ref[c, i] for i in range(OFFSETS)]
        low, high = solve_tree(tree, offsets[CELLS:], *ends[c])
        for k, h in enumerate(solve_chunk(factors, offsets[:CELLS], low, high)):
            turned_ref[c, pl.ds(k, CHUNKS, stride=DEPTH), :] = h
        half_ref[c] = turned_ref[c].T
    for c in range(2):
        factors = load_factors(y_factor_ref, c, CELLS)
        tree = load_factors(y_factor_ref, c, 3, 3 * CELLS)
        sources = [half_ref[c, pl.ds(k, CHUNKS, stride=DEPTH), :] for k in range(DEPTH)]
        offsets, source = source_chunk(factors, sources)
        tree_offsets, source = source_tree(tree, source)
        save(y_offset_ref, c, 0, offsets + tree_offsets)
        source_rows(pay_ref, c, source)
    spread(pay_ref, out_ref)


def finish_kernel(
    gathered_ref, gates_ref, table_ref, y_factor_ref, y_offset_ref, half_ref,
    half_out, advanced_out,
    ring_ref, advanced_ref, sems,
):
    copies = [pltpu.make_async_copy(half_ref, half_out, sems.at[2])]
    copies[0].start()
    ends = outer_ends(
        gathered_ref, gates_ref, table_ref, ring_ref, lax.axis_index("gy"), TURN_Y
    )
    for c in range(2):
        factors = load_factors(y_factor_ref, c, CELLS)
        tree = load_factors(y_factor_ref, c, 3, 3 * CELLS)
        offsets = [y_offset_ref[c, i] for i in range(OFFSETS)]
        low, high = solve_tree(tree, offsets[CELLS:], *ends[c])
        for k, h in enumerate(solve_chunk(factors, offsets[:CELLS], low, high)):
            advanced_ref[c, pl.ds(k, CHUNKS, stride=DEPTH), :] = h
        copies.append(pltpu.make_async_copy(advanced_ref.at[c], advanced_out.at[c], sems.at[c]))
        copies[-1].start()
    for copy in copies:
        copy.wait()


TURN_X = 11
TURN_Y = 10


def turned_exchange(x, axis, turn):
    group = [(i + turn) % DEVICES for i in range(DEVICES)]
    return lax.all_to_all(x, axis, 0, 0, axis_index_groups=[group], tiled=True)


def f32(*shape):
    return jax.ShapeDtypeStruct(shape, jnp.float32)


VMEM = pl.BlockSpec(memory_space=pltpu.VMEM)
HBM = pl.BlockSpec(memory_space=pltpu.HBM)
SPREAD = (DEVICES * SLABS, SLAB, SIDE)
PARAMS = pltpu.CompilerParams(vmem_limit_bytes=8 << 20)
BLOCK = (2, SIDE, SIDE)
FACTORS = (2, STORED, CHUNKS, SIDE)
OFFSET = (2, OFFSETS, CHUNKS, SIDE)


def per_device(fields, material, conduct, joints_x, joints_y):
    inputs = (fields, material, conduct, joints_x.T, joints_y.T)
    with jax.named_scope("reduce_x"):
        pay, x_factor, x_offset, y_factor, y_pay, x_gates, y_gates, table = pl.pallas_call(
            reduce_kernel,
            out_shape=(f32(*SPREAD), f32(*FACTORS), f32(*OFFSET), f32(*FACTORS))
            + (f32(ROWS, SIDE), f32(DEVICES, SIDE), f32(DEVICES, SIDE), f32(2 * MATERIALS, SIDE)),
            in_specs=[HBM] * 5,
            out_specs=(VMEM,) * 8,
            scratch_shapes=[
                pltpu.VMEM(BLOCK, jnp.float32),
                pltpu.VMEM((SIDE, SIDE), jnp.int32),
                pltpu.SMEM(conduct.shape, jnp.float32),
                pltpu.VMEM(joints_x.shape[::-1], jnp.int32),
                pltpu.VMEM(joints_y.shape[::-1], jnp.int32),
                pltpu.VMEM(BLOCK, jnp.float32),
                pltpu.VMEM((SIDE, SIDE), jnp.int32),
                pltpu.VMEM((ROWS, SIDE), jnp.float32),
                pltpu.SemaphoreType.DMA((6,)),
            ],
            compiler_params=PARAMS,
        )(*(pltpu.with_memory_space_constraint(x, pltpu.HBM) for x in inputs))
    with jax.named_scope("exchange_x"):
        gathered = turned_exchange(pay, "gx", TURN_X)
    with jax.named_scope("solve_x_reduce_y"):
        half, pay, y_offset = pl.pallas_call(
            turn_kernel,
            out_shape=(f32(*BLOCK), f32(*SPREAD), f32(*OFFSET)),
            in_specs=[VMEM] * 7,
            out_specs=(VMEM,) * 3,
            scratch_shapes=[
                pltpu.VMEM((DEVICES * ROWS, SIDE), jnp.float32),
                pltpu.VMEM(BLOCK, jnp.float32),
                pltpu.VMEM((ROWS, SIDE), jnp.float32),
            ],
            compiler_params=PARAMS,
        )(gathered, x_gates, table, x_factor, x_offset, y_factor, y_pay)
    with jax.named_scope("exchange_y"):
        gathered = turned_exchange(pay, "gy", TURN_Y)
    with jax.named_scope("solve_y"):
        return pl.pallas_call(
            finish_kernel,
            out_shape=(f32(*BLOCK), f32(*BLOCK)),
            in_specs=[VMEM] * 6,
            out_specs=(HBM, HBM),
            scratch_shapes=[
                pltpu.VMEM((DEVICES * ROWS, SIDE), jnp.float32),
                pltpu.VMEM(BLOCK, jnp.float32),
                pltpu.SemaphoreType.DMA((3,)),
            ],
            compiler_params=PARAMS,
        )(gathered, y_gates, table, y_factor, y_offset, half)


def solution(mesh):
    return jax.shard_map(
        per_device,
        mesh=mesh,
        in_specs=(P(None, "gy", "gx"), P("gy", "gx"), P(), P("gy", None), P("gx", None)),
        out_specs=(P(None, "gy", "gx"), P(None, "gy", "gx")),
        check_vma=False,
    )
```

```python
import jax
import jax.numpy as jnp
from jax import lax
from jax.experimental import pallas as pl
from jax.experimental.pallas import tpu as pltpu
from jax.sharding import PartitionSpec as P

MATERIALS = 8
FOURIER = 8192
DRYING = 4096
HALF_SCALE = (FOURIER * 0.5, DRYING * 0.5)

CHUNKS = 8
DEPTH = 16
SIDE = 128
DEVICES = 16
ROWS = 16
SLABS, SLAB = 6, 2
G_LOW, G_HIGH, LINK, S_LOW, S_HIGH = range(5)
KIND_LOW, KIND_HIGH, OPEN = 10, 11, 12


def sublane():
    return lax.broadcasted_iota(jnp.int32, (CHUNKS, SIDE), 0)


def rolled(x, shift):
    return pltpu.roll(x, shift % CHUNKS, 0)


def chosen(kind, values):
    for b in (1, 2, 4):
        bit = (kind & b) != 0
        values = [jnp.where(bit, values[i + 1], values[i]) for i in range(0, len(values), 2)]
    return values[0]


def conductivities(load, conduct_ref):
    kinds = [load(k) for k in range(DEPTH)]
    return [
        [
            chosen(kind, [conduct_ref[c, q] * HALF_SCALE[c] for q in range(MATERIALS)])
            for kind in kinds
        ]
        for c in range(2)
    ]


def cut_bits(joints_ref, base):
    lane_joints = joints_ref[...] - base
    chunk_start = sublane() * DEPTH
    flags = jnp.zeros((CHUNKS, SIDE), jnp.int32)
    for q in range(joints_ref.shape[0]):
        place = jnp.broadcast_to(lane_joints[q : q + 1, :], (CHUNKS, SIDE)) - chunk_start
        inside = (place >= 0) & (place < DEPTH)
        flags = flags | jnp.where(inside, jnp.left_shift(1, place & (DEPTH - 1)), 0)
    return flags


def face_links(cells, flags):
    links = []
    for k in range(DEPTH):
        before = rolled(cells[DEPTH - 1], 1) if k == 0 else cells[k - 1]
        links.append(jnp.where((flags & (1 << k)) != 0, 0.0, before + cells[k]))
    return links


ORDER = [
    (m, m - half, m + half)
    for half in (1, 2, 4, 8)
    for m in range(half - 1, DEPTH - 1, 2 * half)
]


def factor_chunk(links):
    first = sublane() == 0
    ground = {k: jnp.ones((CHUNKS, SIDE), jnp.float32) for k in range(DEPTH)}
    ground[-1] = jnp.zeros((CHUNKS, SIDE), jnp.float32)
    below = {k: links[k] for k in range(DEPTH)}
    factors = []
    for m, low, high in ORDER:
        a, b, g = below[m], below[high], ground[m]
        inverse = 1.0 / (a + b + g)
        if m == 0:
            inverse = jnp.where(first, 0.0, inverse)
        to_low, to_high = a * inverse, b * inverse
        if m == 0:
            to_low = jnp.where(first, 1.0, to_low)
        ground[low] = ground[low] + to_low * g
        ground[high] = ground[high] + to_high * g
        below[high] = to_low * b
        factors.append((to_low, to_high, inverse))
    return factors, (ground[-1], ground[DEPTH - 1], below[DEPTH - 1])


def source_chunk(factors, sources):
    source = dict(enumerate(sources))
    source[-1] = jnp.zeros((CHUNKS, SIDE), jnp.float32)
    offsets = []
    for (m, low, high), (to_low, to_high, inverse) in zip(ORDER, factors):
        s = source[m]
        source[low] = source[low] + to_low * s
        source[high] = source[high] + to_high * s
        offsets.append(inverse * s)
    return offsets, (source[-1], source[DEPTH - 1])


def join_factor(a, b):
    ground = a[1] + b[0]
    inverse = 1.0 / (a[2] + b[2] + ground)
    to_low, to_high = a[2] * inverse, b[2] * inverse
    joined = (a[0] + to_low * ground, b[1] + to_high * ground, to_low * b[2])
    return (to_low, to_high, inverse), joined


def join_source(factor, a, b):
    to_low, to_high, inverse = factor
    s = a[1] + b[0]
    return inverse * s, (a[0] + to_low * s, b[1] + to_high * s)


def factor_tree(element):
    factors = []
    for step in (1, 2, 4):
        factor, element = join_factor(element, [rolled(x, -step) for x in element])
        factors.append(factor)
    return factors, element


def source_tree(factors, source):
    offsets = []
    for step, factor in zip((1, 2, 4), factors):
        offset, source = join_source(factor, source, [rolled(x, -step) for x in source])
        offsets.append(offset)
    return offsets, source


def solve_tree(factors, offsets, low, high):
    row = sublane()
    for step, (to_low, to_high, _), offset in reversed(list(zip((1, 2, 4), factors, offsets))):
        middle = offset + to_low * low + to_high * high
        upper = (row & step) != 0
        low, high = jnp.where(upper, rolled(middle, step), low), jnp.where(
            upper, rolled(high, step), middle
        )
    return low, high


def solve_chunk(factors, offsets, low, high):
    h = {-1: low, DEPTH - 1: high}
    for (m, lo, hi), (to_low, to_high, _), offset in reversed(list(zip(ORDER, factors, offsets))):
        h[m] = offset + to_low * h[lo] + to_high * h[hi]
    return [h[k] for k in range(DEPTH)]


def gates(joints_ref):
    joints = joints_ref[...]
    flags = jnp.ones((1, SIDE), jnp.int32)
    for q in range(joints_ref.shape[0]):
        joint = joints[q : q + 1, :]
        at_edge = (joint & (SIDE - 1)) == 0
        device = lax.shift_right_logical(joint, SIDE.bit_length() - 1) & (DEVICES - 1)
        flags = flags | jnp.where(at_edge, jnp.left_shift(1, device), 0)
    row = lax.broadcasted_iota(jnp.int32, (DEVICES, SIDE), 0)
    flags = jnp.broadcast_to(flags, (DEVICES, SIDE))
    return jnp.where((lax.shift_right_logical(flags, row) & 1) != 0, 0.0, 1.0)


def outer_ends(gathered_ref, gates_ref, table_ref, ring_ref, me, turn):
    for d in range(DEVICES):
        member = lax.rem(me + (1 + d - turn) % DEVICES, DEVICES)
        for p in range(SLABS):
            at = d * ROWS + p * SLAB
            ring_ref[at : at + SLAB, :] = gathered_ref[SLABS * member + p]
        device = lax.rem(me + 1 + d, DEVICES)
        ring_ref[d * ROWS + OPEN : d * ROWS + OPEN + 1, :] = gates_ref[pl.ds(device, 1), :]
    own = sublane() == CHUNKS - 1

    def part(row, odd):
        return ring_ref[pl.ds(odd * ROWS + row, 8, stride=2 * ROWS), :]

    kinds_low, kinds_high = (
        [part(row, odd).astype(jnp.int32) for odd in range(2)] for row in (KIND_LOW, KIND_HIGH)
    )
    ends = []
    for c in range(2):
        values = [
            jnp.broadcast_to(table_ref[MATERIALS * c + q : MATERIALS * c + q + 1, :], own.shape)
            for q in range(MATERIALS)
        ]
        cells_low, cells_high = (
            [chosen(kind, values) for kind in kinds] for kinds in (kinds_low, kinds_high)
        )
        elements, sources = [], []
        for odd in range(2):
            before = cells_high[0] if odd else rolled(cells_high[1], 1)
            entry = (before + cells_low[odd]) * part(OPEN, odd)
            zero = jnp.zeros_like(entry)
            factor, element = join_factor(
                (zero, zero, entry), [part(2 * q + c, odd) for q in (G_LOW, G_HIGH, LINK)]
            )
            _, source = join_source(
                factor, (zero, zero), [part(2 * q + c, odd) for q in (S_LOW, S_HIGH)]
            )
            if odd:
                element = [
                    jnp.where(own, y, x) for x, y in zip(element, (zero, zero, entry))
                ]
                source = [jnp.where(own, 0.0, x) for x in source]
            elements.append(element)
            sources.append(source)
        factor, element = join_factor(*elements)
        _, source = join_source(factor, *sources)
        factors, element = factor_tree(element)
        _, source = source_tree(factors, source)

        def mine(q):
            at = (DEVICES - 1) * ROWS + 2 * q + c
            return ring_ref[at : at + 1, :]

        g_low = mine(G_LOW) + element[1][0:1, :]
        g_high = mine(G_HIGH) + element[0][0:1, :]
        link = mine(LINK) + element[2][0:1, :]
        s_low = mine(S_LOW) + source[1][0:1, :]
        s_high = mine(S_HIGH) + source[0][0:1, :]
        inverse = 1.0 / (g_low * g_high + link * (g_low + g_high))
        low = (s_low * (g_high + link) + link * s_high) * inverse
        high = (s_high * (g_low + link) + link * s_low) * inverse
        ends.append(
            (jnp.broadcast_to(low, (CHUNKS, SIDE)), jnp.broadcast_to(high, (CHUNKS, SIDE)))
        )
    return ends


def save(ref, c, at, values):
    for i, x in enumerate(values):
        ref[c, at + i] = x


def load_factors(ref, c, count, at=0):
    return [tuple(ref[c, at + 3 * i + j] for j in range(3)) for i in range(count)]


CELLS = len(ORDER)
STORED = 3 * CELLS + 9
OFFSETS = CELLS + 3


def flatten(factors):
    return [x for factor in factors for x in factor]


def put(pay_ref, row, x):
    pay_ref[row : row + 1, :] = x


def static_rows(pay_ref, c, element):
    for q, x in zip((G_LOW, G_HIGH, LINK), element):
        put(pay_ref, 2 * q + c, x[0:1, :])


def kind_rows(pay_ref, kind_ref):
    for row, at in ((KIND_LOW, 0), (KIND_HIGH, SIDE - 1)):
        put(pay_ref, row, kind_ref[at : at + 1, :].astype(jnp.float32))


def source_rows(pay_ref, c, source):
    for q, x in zip((S_LOW, S_HIGH), source):
        put(pay_ref, 2 * q + c, x[0:1, :])


def spread(pay_ref, out_ref):
    for p in range(SLABS):
        slab = pay_ref[p * SLAB : (p + 1) * SLAB, :]
        for d in range(DEVICES):
            out_ref[SLABS * d + p] = slab


def reduce_kernel(
    fields_in, material_in, conduct_in, joints_x_in, joints_y_in,
    out_ref, x_factor_ref, x_offset_ref, y_factor_ref, y_pay_ref,
    x_gates_ref, y_gates_ref, table_ref,
    fields_ref, material_ref, conduct_ref, joints_x_ref, joints_y_ref,
    turned_ref, kind_ref, pay_ref, sems,
):
    at_x, at_y = lax.axis_index("gx"), lax.axis_index("gy")
    copies = [
        pltpu.make_async_copy(source, target, sems.at[i])
        for i, (source, target) in enumerate(
            (
                (material_in, material_ref),
                (conduct_in, conduct_ref),
                (joints_x_in, joints_x_ref),
                (joints_y_in, joints_y_ref),
                (fields_in, fields_ref),
            )
        )
    ]
    for copy in copies:
        copy.start()
    for copy in copies[:4]:
        copy.wait()
    kind_ref[...] = material_ref[...].T
    flags = cut_bits(joints_x_ref, at_x * SIDE)
    cells = conductivities(lambda k: kind_ref[pl.ds(k, CHUNKS, stride=DEPTH), :], conduct_ref)
    chunks = [factor_chunk(face_links(cells[c], flags)) for c in range(2)]
    trees = [factor_tree(element) for _, element in chunks]
    kind_rows(pay_ref, kind_ref)
    for c in range(2):
        static_rows(pay_ref, c, trees[c][1])
        save(x_factor_ref, c, 0, flatten(chunks[c][0] + trees[c][0]))
    copies[4].wait()
    for c in range(2):
        turned_ref[c] = fields_ref[c].T
        sources = [turned_ref[c, pl.ds(k, CHUNKS, stride=DEPTH), :] for k in range(DEPTH)]
        offsets, source = source_chunk(chunks[c][0], sources)
        tree_offsets, source = source_tree(trees[c][0], source)
        save(x_offset_ref, c, 0, offsets + tree_offsets)
        source_rows(pay_ref, c, source)
    spread(pay_ref, out_ref)
    x_gates_ref[...] = gates(joints_x_ref)
    y_gates_ref[...] = gates(joints_y_ref)
    for c in range(2):
        for q in range(MATERIALS):
            table_ref[MATERIALS * c + q : MATERIALS * c + q + 1, :] = jnp.full(
                (1, SIDE), conduct_ref[c, q] * HALF_SCALE[c], jnp.float32
            )
    flags = cut_bits(joints_y_ref, at_y * SIDE)
    cells = conductivities(lambda k: material_ref[pl.ds(k, CHUNKS, stride=DEPTH), :], conduct_ref)
    y_pay_ref[...] = jnp.zeros_like(y_pay_ref)
    kind_rows(y_pay_ref, material_ref)
    for c in range(2):
        factors, element = factor_chunk(face_links(cells[c], flags))
        tree, element = factor_tree(element)
        save(y_factor_ref, c, 0, flatten(factors + tree))
        static_rows(y_pay_ref, c, element)


def turn_kernel(
    gathered_ref, gates_ref, table_ref, x_factor_ref, x_offset_ref, y_factor_ref, y_pay_ref,
    half_ref, out_ref, y_offset_ref,
    ring_ref, turned_ref, pay_ref,
):
    ends = outer_ends(
        gathered_ref, gates_ref, table_ref, ring_ref, lax.axis_index("gx"), TURN_X
    )
    pay_ref[...] = y_pay_ref[...]
    for c in range(2):
        factors = load_factors(x_factor_ref, c, CELLS)
        tree = load_factors(x_factor_ref, c, 3, 3 * CELLS)
        offsets = [x_offset_ref[c, i] for i in range(OFFSETS)]
        low, high = solve_tree(tree, offsets[CELLS:], *ends[c])
        for k, h in enumerate(solve_chunk(factors, offsets[:CELLS], low, high)):
            turned_ref[c, pl.ds(k, CHUNKS, stride=DEPTH), :] = h
        half_ref[c] = turned_ref[c].T
    for c in range(2):
        factors = load_factors(y_factor_ref, c, CELLS)
        tree = load_factors(y_factor_ref, c, 3, 3 * CELLS)
        sources = [half_ref[c, pl.ds(k, CHUNKS, stride=DEPTH), :] for k in range(DEPTH)]
        offsets, source = source_chunk(factors, sources)
        tree_offsets, source = source_tree(tree, source)
        save(y_offset_ref, c, 0, offsets + tree_offsets)
        source_rows(pay_ref, c, source)
    spread(pay_ref, out_ref)


def finish_kernel(
    gathered_ref, gates_ref, table_ref, y_factor_ref, y_offset_ref, half_ref,
    half_out, advanced_out,
    ring_ref, advanced_ref, sems,
):
    copies = [pltpu.make_async_copy(half_ref, half_out, sems.at[2])]
    copies[0].start()
    ends = outer_ends(
        gathered_ref, gates_ref, table_ref, ring_ref, lax.axis_index("gy"), TURN_Y
    )
    for c in range(2):
        factors = load_factors(y_factor_ref, c, CELLS)
        tree = load_factors(y_factor_ref, c, 3, 3 * CELLS)
        offsets = [y_offset_ref[c, i] for i in range(OFFSETS)]
        low, high = solve_tree(tree, offsets[CELLS:], *ends[c])
        for k, h in enumerate(solve_chunk(factors, offsets[:CELLS], low, high)):
            advanced_ref[c, pl.ds(k, CHUNKS, stride=DEPTH), :] = h
        copies.append(pltpu.make_async_copy(advanced_ref.at[c], advanced_out.at[c], sems.at[c]))
        copies[-1].start()
    for copy in copies:
        copy.wait()


TURN_X = 11
TURN_Y = 10


def turned_exchange(x, axis, turn):
    group = [(i + turn) % DEVICES for i in range(DEVICES)]
    return lax.all_to_all(x, axis, 0, 0, axis_index_groups=[group], tiled=True)


def f32(*shape):
    return jax.ShapeDtypeStruct(shape, jnp.float32)


VMEM = pl.BlockSpec(memory_space=pltpu.VMEM)
HBM = pl.BlockSpec(memory_space=pltpu.HBM)
SPREAD = (DEVICES * SLABS, SLAB, SIDE)
PARAMS = pltpu.CompilerParams(vmem_limit_bytes=8 << 20)
BLOCK = (2, SIDE, SIDE)
FACTORS = (2, STORED, CHUNKS, SIDE)
OFFSET = (2, OFFSETS, CHUNKS, SIDE)


def per_device(fields, material, conduct, joints_x, joints_y):
    inputs = (fields, material, conduct, joints_x.T, joints_y.T)
    with jax.named_scope("reduce_x"):
        pay, x_factor, x_offset, y_factor, y_pay, x_gates, y_gates, table = pl.pallas_call(
            reduce_kernel,
            out_shape=(f32(*SPREAD), f32(*FACTORS), f32(*OFFSET), f32(*FACTORS))
            + (f32(ROWS, SIDE), f32(DEVICES, SIDE), f32(DEVICES, SIDE), f32(2 * MATERIALS, SIDE)),
            in_specs=[HBM] * 5,
            out_specs=(VMEM,) * 8,
            scratch_shapes=[
                pltpu.VMEM(BLOCK, jnp.float32),
                pltpu.VMEM((SIDE, SIDE), jnp.int32),
                pltpu.SMEM(conduct.shape, jnp.float32),
                pltpu.VMEM(joints_x.shape[::-1], jnp.int32),
                pltpu.VMEM(joints_y.shape[::-1], jnp.int32),
                pltpu.VMEM(BLOCK, jnp.float32),
                pltpu.VMEM((SIDE, SIDE), jnp.int32),
                pltpu.VMEM((ROWS, SIDE), jnp.float32),
                pltpu.SemaphoreType.DMA((5,)),
            ],
            compiler_params=PARAMS,
        )(*(pltpu.with_memory_space_constraint(x, pltpu.HBM) for x in inputs))
    with jax.named_scope("exchange_x"):
        gathered = turned_exchange(pay, "gx", TURN_X)
    with jax.named_scope("solve_x_reduce_y"):
        half, pay, y_offset = pl.pallas_call(
            turn_kernel,
            out_shape=(f32(*BLOCK), f32(*SPREAD), f32(*OFFSET)),
            in_specs=[VMEM] * 7,
            out_specs=(VMEM,) * 3,
            scratch_shapes=[
                pltpu.VMEM((DEVICES * ROWS, SIDE), jnp.float32),
                pltpu.VMEM(BLOCK, jnp.float32),
                pltpu.VMEM((ROWS, SIDE), jnp.float32),
            ],
            compiler_params=PARAMS,
        )(gathered, x_gates, table, x_factor, x_offset, y_factor, y_pay)
    with jax.named_scope("exchange_y"):
        gathered = turned_exchange(pay, "gy", TURN_Y)
    with jax.named_scope("solve_y"):
        return pl.pallas_call(
            finish_kernel,
            out_shape=(f32(*BLOCK), f32(*BLOCK)),
            in_specs=[VMEM] * 6,
            out_specs=(HBM, HBM),
            scratch_shapes=[
                pltpu.VMEM((DEVICES * ROWS, SIDE), jnp.float32),
                pltpu.VMEM(BLOCK, jnp.float32),
                pltpu.SemaphoreType.DMA((3,)),
            ],
            compiler_params=PARAMS,
        )(gathered, y_gates, table, y_factor, y_offset, half)


def solution(mesh):
    return jax.shard_map(
        per_device,
        mesh=mesh,
        in_specs=(P(None, "gy", "gx"), P("gy", "gx"), P(), P("gy", None), P("gx", None)),
        out_specs=(P(None, "gy", "gx"), P(None, "gy", "gx")),
        check_vma=False,
    )
```

```python
import jax
import jax.numpy as jnp
from jax import lax
from jax.experimental import pallas as pl
from jax.experimental.pallas import tpu as pltpu
from jax.sharding import PartitionSpec as P

MATERIALS = 8
FOURIER = 8192
DRYING = 4096
HALF_SCALE = (FOURIER * 0.5, DRYING * 0.5)

CHUNKS = 8
DEPTH = 16
SIDE = 128
DEVICES = 16
ROWS = 16
SLABS, SLAB = 6, 2
G_LOW, G_HIGH, LINK, S_LOW, S_HIGH = range(5)
KIND_LOW, KIND_HIGH, OPEN = 10, 11, 12


def sublane():
    return lax.broadcasted_iota(jnp.int32, (CHUNKS, SIDE), 0)


def rolled(x, shift):
    return pltpu.roll(x, shift % CHUNKS, 0)


def chosen(kind, values):
    for b in (1, 2, 4):
        bit = (kind & b) != 0
        values = [jnp.where(bit, values[i + 1], values[i]) for i in range(0, len(values), 2)]
    return values[0]


def over_chunks(row):
    return jnp.broadcast_to(row, (CHUNKS, SIDE))


def conductivities(load, value):
    kinds = [load(k) for k in range(DEPTH)]
    return [
        [
            chosen(kind, [value(c, q) for q in range(MATERIALS)])
            for kind in kinds
        ]
        for c in range(2)
    ]


def cut_bits(joints_ref, base):
    lane_joints = joints_ref[...] - base
    chunk_start = sublane() * DEPTH
    flags = jnp.zeros((CHUNKS, SIDE), jnp.int32)
    for q in range(joints_ref.shape[0]):
        place = jnp.broadcast_to(lane_joints[q : q + 1, :], (CHUNKS, SIDE)) - chunk_start
        inside = (place >= 0) & (place < DEPTH)
        flags = flags | jnp.where(inside, jnp.left_shift(1, place & (DEPTH - 1)), 0)
    return flags


def face_links(cells, flags):
    links = []
    for k in range(DEPTH):
        before = rolled(cells[DEPTH - 1], 1) if k == 0 else cells[k - 1]
        links.append(jnp.where((flags & (1 << k)) != 0, 0.0, before + cells[k]))
    return links


ORDER = [
    (m, m - half, m + half)
    for half in (1, 2, 4, 8)
    for m in range(half - 1, DEPTH - 1, 2 * half)
]


def factor_chunk(links):
    first = sublane() == 0
    ground = {k: jnp.ones((CHUNKS, SIDE), jnp.float32) for k in range(DEPTH)}
    ground[-1] = jnp.zeros((CHUNKS, SIDE), jnp.float32)
    below = {k: links[k] for k in range(DEPTH)}
    factors = []
    for m, low, high in ORDER:
        a, b, g = below[m], below[high], ground[m]
        inverse = 1.0 / (a + b + g)
        if m == 0:
            inverse = jnp.where(first, 0.0, inverse)
        to_low, to_high = a * inverse, b * inverse
        if m == 0:
            to_low = jnp.where(first, 1.0, to_low)
        ground[low] = ground[low] + to_low * g
        ground[high] = ground[high] + to_high * g
        below[high] = to_low * b
        factors.append((to_low, to_high, inverse))
    return factors, (ground[-1], ground[DEPTH - 1], below[DEPTH - 1])


def source_chunk(factors, sources):
    source = dict(enumerate(sources))
    source[-1] = jnp.zeros((CHUNKS, SIDE), jnp.float32)
    offsets = []
    for (m, low, high), (to_low, to_high, inverse) in zip(ORDER, factors):
        s = source[m]
        source[low] = source[low] + to_low * s
        source[high] = source[high] + to_high * s
        offsets.append(inverse * s)
    return offsets, (source[-1], source[DEPTH - 1])


def join_factor(a, b):
    ground = a[1] + b[0]
    inverse = 1.0 / (a[2] + b[2] + ground)
    to_low, to_high = a[2] * inverse, b[2] * inverse
    joined = (a[0] + to_low * ground, b[1] + to_high * ground, to_low * b[2])
    return (to_low, to_high, inverse), joined


def join_source(factor, a, b):
    to_low, to_high, inverse = factor
    s = a[1] + b[0]
    return inverse * s, (a[0] + to_low * s, b[1] + to_high * s)


def factor_tree(element):
    factors = []
    for step in (1, 2, 4):
        factor, element = join_factor(element, [rolled(x, -step) for x in element])
        factors.append(factor)
    return factors, element


def source_tree(factors, source):
    offsets = []
    for step, factor in zip((1, 2, 4), factors):
        offset, source = join_source(factor, source, [rolled(x, -step) for x in source])
        offsets.append(offset)
    return offsets, source


def solve_tree(factors, offsets, low, high):
    row = sublane()
    for step, (to_low, to_high, _), offset in reversed(list(zip((1, 2, 4), factors, offsets))):
        middle = offset + to_low * low + to_high * high
        upper = (row & step) != 0
        low, high = jnp.where(upper, rolled(middle, step), low), jnp.where(
            upper, rolled(high, step), middle
        )
    return low, high


def solve_chunk(factors, offsets, low, high):
    h = {-1: low, DEPTH - 1: high}
    for (m, lo, hi), (to_low, to_high, _), offset in reversed(list(zip(ORDER, factors, offsets))):
        h[m] = offset + to_low * h[lo] + to_high * h[hi]
    return [h[k] for k in range(DEPTH)]


def gates(joints_ref):
    joints = joints_ref[...]
    flags = jnp.ones((1, SIDE), jnp.int32)
    for q in range(joints_ref.shape[0]):
        joint = joints[q : q + 1, :]
        at_edge = (joint & (SIDE - 1)) == 0
        device = lax.shift_right_logical(joint, SIDE.bit_length() - 1) & (DEVICES - 1)
        flags = flags | jnp.where(at_edge, jnp.left_shift(1, device), 0)
    row = lax.broadcasted_iota(jnp.int32, (DEVICES, SIDE), 0)
    flags = jnp.broadcast_to(flags, (DEVICES, SIDE))
    return jnp.where((lax.shift_right_logical(flags, row) & 1) != 0, 0.0, 1.0)


def outer_ends(gathered_ref, gates_ref, table_ref, ring_ref, me, turn):
    for d in range(DEVICES):
        member = lax.rem(me + (1 + d - turn) % DEVICES, DEVICES)
        for p in range(SLABS):
            at = d * ROWS + p * SLAB
            ring_ref[at : at + SLAB, :] = gathered_ref[SLABS * member + p]
        device = lax.rem(me + 1 + d, DEVICES)
        ring_ref[d * ROWS + OPEN : d * ROWS + OPEN + 1, :] = gates_ref[pl.ds(device, 1), :]
    own = sublane() == CHUNKS - 1

    def part(row, odd):
        return ring_ref[pl.ds(odd * ROWS + row, 8, stride=2 * ROWS), :]

    kinds_low, kinds_high = (
        [part(row, odd).astype(jnp.int32) for odd in range(2)] for row in (KIND_LOW, KIND_HIGH)
    )
    ends = []
    for c in range(2):
        values = [
            jnp.broadcast_to(table_ref[MATERIALS * c + q : MATERIALS * c + q + 1, :], own.shape)
            for q in range(MATERIALS)
        ]
        cells_low, cells_high = (
            [chosen(kind, values) for kind in kinds] for kinds in (kinds_low, kinds_high)
        )
        elements, sources = [], []
        for odd in range(2):
            before = cells_high[0] if odd else rolled(cells_high[1], 1)
            entry = (before + cells_low[odd]) * part(OPEN, odd)
            zero = jnp.zeros_like(entry)
            factor, element = join_factor(
                (zero, zero, entry), [part(2 * q + c, odd) for q in (G_LOW, G_HIGH, LINK)]
            )
            _, source = join_source(
                factor, (zero, zero), [part(2 * q + c, odd) for q in (S_LOW, S_HIGH)]
            )
            if odd:
                element = [
                    jnp.where(own, y, x) for x, y in zip(element, (zero, zero, entry))
                ]
                source = [jnp.where(own, 0.0, x) for x in source]
            elements.append(element)
            sources.append(source)
        factor, element = join_factor(*elements)
        _, source = join_source(factor, *sources)
        factors, element = factor_tree(element)
        _, source = source_tree(factors, source)

        def mine(q):
            at = (DEVICES - 1) * ROWS + 2 * q + c
            return ring_ref[at : at + 1, :]

        g_low = mine(G_LOW) + element[1][0:1, :]
        g_high = mine(G_HIGH) + element[0][0:1, :]
        link = mine(LINK) + element[2][0:1, :]
        s_low = mine(S_LOW) + source[1][0:1, :]
        s_high = mine(S_HIGH) + source[0][0:1, :]
        inverse = 1.0 / (g_low * g_high + link * (g_low + g_high))
        low = (s_low * (g_high + link) + link * s_high) * inverse
        high = (s_high * (g_low + link) + link * s_low) * inverse
        ends.append(
            (jnp.broadcast_to(low, (CHUNKS, SIDE)), jnp.broadcast_to(high, (CHUNKS, SIDE)))
        )
    return ends


def save(ref, c, at, values):
    for i, x in enumerate(values):
        ref[c, at + i] = x


def load_factors(ref, c, count, at=0):
    return [tuple(ref[c, at + 3 * i + j] for j in range(3)) for i in range(count)]


CELLS = len(ORDER)
STORED = 3 * CELLS + 9
OFFSETS = CELLS + 3


def flatten(factors):
    return [x for factor in factors for x in factor]


def put(pay_ref, row, x):
    pay_ref[row : row + 1, :] = x


def static_rows(pay_ref, c, element):
    for q, x in zip((G_LOW, G_HIGH, LINK), element):
        put(pay_ref, 2 * q + c, x[0:1, :])


def kind_rows(pay_ref, kind_ref):
    for row, at in ((KIND_LOW, 0), (KIND_HIGH, SIDE - 1)):
        put(pay_ref, row, kind_ref[at : at + 1, :].astype(jnp.float32))


def source_rows(pay_ref, c, source):
    for q, x in zip((S_LOW, S_HIGH), source):
        put(pay_ref, 2 * q + c, x[0:1, :])


def spread(pay_ref, out_ref):
    for p in range(SLABS):
        slab = pay_ref[p * SLAB : (p + 1) * SLAB, :]
        for d in range(DEVICES):
            out_ref[SLABS * d + p] = slab


def reduce_kernel(
    fields_in, material_in, conduct_in, joints_x_in, joints_y_in,
    out_ref, x_factor_ref, x_offset_ref, x_gates_ref, table_ref, material_ref, joints_y_ref,
    fields_ref, conduct_ref, joints_x_ref,
    turned_ref, kind_ref, pay_ref, sems,
):
    at_x = lax.axis_index("gx")
    copies = [
        pltpu.make_async_copy(source, target, sems.at[i])
        for i, (source, target) in enumerate(
            (
                (material_in, material_ref),
                (conduct_in, conduct_ref),
                (joints_x_in, joints_x_ref),
                (joints_y_in, joints_y_ref),
                (fields_in, fields_ref),
            )
        )
    ]
    for copy in copies:
        copy.start()
    for copy in copies[:4]:
        copy.wait()
    kind_ref[...] = material_ref[...].T
    flags = cut_bits(joints_x_ref, at_x * SIDE)
    cells = conductivities(
        lambda k: kind_ref[pl.ds(k, CHUNKS, stride=DEPTH), :],
        lambda c, q: conduct_ref[c, q] * HALF_SCALE[c],
    )
    chunks = [factor_chunk(face_links(cells[c], flags)) for c in range(2)]
    trees = [factor_tree(element) for _, element in chunks]
    kind_rows(pay_ref, kind_ref)
    for c in range(2):
        static_rows(pay_ref, c, trees[c][1])
        save(x_factor_ref, c, 0, flatten(chunks[c][0] + trees[c][0]))
    copies[4].wait()
    for c in range(2):
        turned_ref[c] = fields_ref[c].T
        sources = [turned_ref[c, pl.ds(k, CHUNKS, stride=DEPTH), :] for k in range(DEPTH)]
        offsets, source = source_chunk(chunks[c][0], sources)
        tree_offsets, source = source_tree(trees[c][0], source)
        save(x_offset_ref, c, 0, offsets + tree_offsets)
        source_rows(pay_ref, c, source)
    spread(pay_ref, out_ref)
    x_gates_ref[...] = gates(joints_x_ref)
    for c in range(2):
        for q in range(MATERIALS):
            table_ref[MATERIALS * c + q : MATERIALS * c + q + 1, :] = jnp.full(
                (1, SIDE), conduct_ref[c, q] * HALF_SCALE[c], jnp.float32
            )


def turn_kernel(
    gathered_ref, gates_ref, table_ref, x_factor_ref, x_offset_ref, material_ref, joints_y_ref,
    half_ref, out_ref, y_factor_ref, y_offset_ref, y_gates_ref,
    ring_ref, turned_ref, pay_ref,
):
    ends = outer_ends(
        gathered_ref, gates_ref, table_ref, ring_ref, lax.axis_index("gx"), TURN_X
    )
    y_gates_ref[...] = gates(joints_y_ref)
    flags = cut_bits(joints_y_ref, lax.axis_index("gy") * SIDE)
    cells = conductivities(
        lambda k: material_ref[pl.ds(k, CHUNKS, stride=DEPTH), :],
        lambda c, q: over_chunks(table_ref[MATERIALS * c + q : MATERIALS * c + q + 1, :]),
    )
    kind_rows(pay_ref, material_ref)
    y_factors = []
    for c in range(2):
        factors, element = factor_chunk(face_links(cells[c], flags))
        tree, element = factor_tree(element)
        y_factors.append((factors, tree))
        save(y_factor_ref, c, 0, flatten(factors + tree))
        static_rows(pay_ref, c, element)
    for c in range(2):
        factors = load_factors(x_factor_ref, c, CELLS)
        tree = load_factors(x_factor_ref, c, 3, 3 * CELLS)
        offsets = [x_offset_ref[c, i] for i in range(OFFSETS)]
        low, high = solve_tree(tree, offsets[CELLS:], *ends[c])
        for k, h in enumerate(solve_chunk(factors, offsets[:CELLS], low, high)):
            turned_ref[c, pl.ds(k, CHUNKS, stride=DEPTH), :] = h
        half_ref[c] = turned_ref[c].T
    for c in range(2):
        factors, tree = y_factors[c]
        sources = [half_ref[c, pl.ds(k, CHUNKS, stride=DEPTH), :] for k in range(DEPTH)]
        offsets, source = source_chunk(factors, sources)
        tree_offsets, source = source_tree(tree, source)
        save(y_offset_ref, c, 0, offsets + tree_offsets)
        source_rows(pay_ref, c, source)
    spread(pay_ref, out_ref)


def finish_kernel(
    gathered_ref, gates_ref, table_ref, y_factor_ref, y_offset_ref, half_ref,
    half_out, advanced_out,
    ring_ref, advanced_ref, sems,
):
    copies = [pltpu.make_async_copy(half_ref, half_out, sems.at[2])]
    copies[0].start()
    ends = outer_ends(
        gathered_ref, gates_ref, table_ref, ring_ref, lax.axis_index("gy"), TURN_Y
    )
    for c in range(2):
        factors = load_factors(y_factor_ref, c, CELLS)
        tree = load_factors(y_factor_ref, c, 3, 3 * CELLS)
        offsets = [y_offset_ref[c, i] for i in range(OFFSETS)]
        low, high = solve_tree(tree, offsets[CELLS:], *ends[c])
        for k, h in enumerate(solve_chunk(factors, offsets[:CELLS], low, high)):
            advanced_ref[c, pl.ds(k, CHUNKS, stride=DEPTH), :] = h
        copies.append(pltpu.make_async_copy(advanced_ref.at[c], advanced_out.at[c], sems.at[c]))
        copies[-1].start()
    for copy in copies:
        copy.wait()


TURN_X = 11
TURN_Y = 10


def turned_exchange(x, axis, turn):
    group = [(i + turn) % DEVICES for i in range(DEVICES)]
    return lax.all_to_all(x, axis, 0, 0, axis_index_groups=[group], tiled=True)


def i32(*shape):
    return jax.ShapeDtypeStruct(shape, jnp.int32)


def f32(*shape):
    return jax.ShapeDtypeStruct(shape, jnp.float32)


VMEM = pl.BlockSpec(memory_space=pltpu.VMEM)
HBM = pl.BlockSpec(memory_space=pltpu.HBM)
SPREAD = (DEVICES * SLABS, SLAB, SIDE)
PARAMS = pltpu.CompilerParams(vmem_limit_bytes=8 << 20)
BLOCK = (2, SIDE, SIDE)
FACTORS = (2, STORED, CHUNKS, SIDE)
OFFSET = (2, OFFSETS, CHUNKS, SIDE)


def per_device(fields, material, conduct, joints_x, joints_y):
    inputs = (fields, material, conduct, joints_x.T, joints_y.T)
    with jax.named_scope("reduce_x"):
        pay, x_factor, x_offset, x_gates, table, kinds, joints = pl.pallas_call(
            reduce_kernel,
            out_shape=(f32(*SPREAD), f32(*FACTORS), f32(*OFFSET), f32(DEVICES, SIDE))
            + (f32(2 * MATERIALS, SIDE), i32(SIDE, SIDE), i32(*joints_y.shape[::-1])),
            in_specs=[HBM] * 5,
            out_specs=(VMEM,) * 7,
            scratch_shapes=[
                pltpu.VMEM(BLOCK, jnp.float32),
                pltpu.SMEM(conduct.shape, jnp.float32),
                pltpu.VMEM(joints_x.shape[::-1], jnp.int32),
                pltpu.VMEM(BLOCK, jnp.float32),
                pltpu.VMEM((SIDE, SIDE), jnp.int32),
                pltpu.VMEM((ROWS, SIDE), jnp.float32),
                pltpu.SemaphoreType.DMA((5,)),
            ],
            compiler_params=PARAMS,
        )(*(pltpu.with_memory_space_constraint(x, pltpu.HBM) for x in inputs))
    with jax.named_scope("exchange_x"):
        gathered = turned_exchange(pay, "gx", TURN_X)
    with jax.named_scope("solve_x_reduce_y"):
        half, pay, y_factor, y_offset, y_gates = pl.pallas_call(
            turn_kernel,
            out_shape=(f32(*BLOCK), f32(*SPREAD), f32(*FACTORS), f32(*OFFSET), f32(DEVICES, SIDE)),
            in_specs=[VMEM] * 7,
            out_specs=(VMEM,) * 5,
            scratch_shapes=[
                pltpu.VMEM((DEVICES * ROWS, SIDE), jnp.float32),
                pltpu.VMEM(BLOCK, jnp.float32),
                pltpu.VMEM((ROWS, SIDE), jnp.float32),
            ],
            compiler_params=PARAMS,
        )(gathered, x_gates, table, x_factor, x_offset, kinds, joints)
    with jax.named_scope("exchange_y"):
        gathered = turned_exchange(pay, "gy", TURN_Y)
    with jax.named_scope("solve_y"):
        return pl.pallas_call(
            finish_kernel,
            out_shape=(f32(*BLOCK), f32(*BLOCK)),
            in_specs=[VMEM] * 6,
            out_specs=(HBM, HBM),
            scratch_shapes=[
                pltpu.VMEM((DEVICES * ROWS, SIDE), jnp.float32),
                pltpu.VMEM(BLOCK, jnp.float32),
                pltpu.SemaphoreType.DMA((3,)),
            ],
            compiler_params=PARAMS,
        )(gathered, y_gates, table, y_factor, y_offset, half)


def solution(mesh):
    return jax.shard_map(
        per_device,
        mesh=mesh,
        in_specs=(P(None, "gy", "gx"), P("gy", "gx"), P(), P("gy", None), P("gx", None)),
        out_specs=(P(None, "gy", "gx"), P(None, "gy", "gx")),
        check_vma=False,
    )
```

```python
import jax
import jax.numpy as jnp
from jax import lax
from jax.experimental import pallas as pl
from jax.experimental.pallas import tpu as pltpu
from jax.sharding import PartitionSpec as P

MATERIALS = 8
FOURIER = 8192
DRYING = 4096
HALF_SCALE = (FOURIER * 0.5, DRYING * 0.5)

CHUNKS = 8
DEPTH = 16
SIDE = 128
DEVICES = 16
ROWS = 16
SLABS, SLAB = 6, 2
G_LOW, G_HIGH, LINK, S_LOW, S_HIGH = range(5)
KIND_LOW, KIND_HIGH, OPEN = 10, 11, 12


def sublane():
    return lax.broadcasted_iota(jnp.int32, (CHUNKS, SIDE), 0)


def rolled(x, shift):
    return pltpu.roll(x, shift % CHUNKS, 0)


def chosen(kind, values):
    for b in (1, 2, 4):
        bit = (kind & b) != 0
        values = [jnp.where(bit, values[i + 1], values[i]) for i in range(0, len(values), 2)]
    return values[0]


def conductivities(load, conduct_ref):
    kinds = [load(k) for k in range(DEPTH)]
    return [
        [
            chosen(kind, [conduct_ref[c, q] * HALF_SCALE[c] for q in range(MATERIALS)])
            for kind in kinds
        ]
        for c in range(2)
    ]


def cut_bits(joints_ref, base):
    lane_joints = joints_ref[...] - base
    chunk_start = sublane() * DEPTH
    flags = jnp.zeros((CHUNKS, SIDE), jnp.int32)
    for q in range(joints_ref.shape[0]):
        place = jnp.broadcast_to(lane_joints[q : q + 1, :], (CHUNKS, SIDE)) - chunk_start
        inside = (place >= 0) & (place < DEPTH)
        flags = flags | jnp.where(inside, jnp.left_shift(1, place & (DEPTH - 1)), 0)
    return flags


def face_links(cells, flags):
    links = []
    for k in range(DEPTH):
        before = rolled(cells[DEPTH - 1], 1) if k == 0 else cells[k - 1]
        links.append(jnp.where((flags & (1 << k)) != 0, 0.0, before + cells[k]))
    return links


ORDER = [
    (m, m - half, m + half)
    for half in (1, 2, 4, 8)
    for m in range(half - 1, DEPTH - 1, 2 * half)
]


def factor_chunk(links):
    first = sublane() == 0
    ground = {k: jnp.ones((CHUNKS, SIDE), jnp.float32) for k in range(DEPTH)}
    ground[-1] = jnp.zeros((CHUNKS, SIDE), jnp.float32)
    below = {k: links[k] for k in range(DEPTH)}
    factors = []
    for m, low, high in ORDER:
        a, b, g = below[m], below[high], ground[m]
        inverse = 1.0 / (a + b + g)
        if m == 0:
            inverse = jnp.where(first, 0.0, inverse)
        to_low, to_high = a * inverse, b * inverse
        if m == 0:
            to_low = jnp.where(first, 1.0, to_low)
        ground[low] = ground[low] + to_low * g
        ground[high] = ground[high] + to_high * g
        below[high] = to_low * b
        factors.append((to_low, to_high, inverse))
    return factors, (ground[-1], ground[DEPTH - 1], below[DEPTH - 1])


def source_chunk(factors, sources):
    source = dict(enumerate(sources))
    source[-1] = jnp.zeros((CHUNKS, SIDE), jnp.float32)
    offsets = []
    for (m, low, high), (to_low, to_high, inverse) in zip(ORDER, factors):
        s = source[m]
        source[low] = source[low] + to_low * s
        source[high] = source[high] + to_high * s
        offsets.append(inverse * s)
    return offsets, (source[-1], source[DEPTH - 1])


def join_factor(a, b):
    ground = a[1] + b[0]
    inverse = 1.0 / (a[2] + b[2] + ground)
    to_low, to_high = a[2] * inverse, b[2] * inverse
    joined = (a[0] + to_low * ground, b[1] + to_high * ground, to_low * b[2])
    return (to_low, to_high, inverse), joined


def join_source(factor, a, b):
    to_low, to_high, inverse = factor
    s = a[1] + b[0]
    return inverse * s, (a[0] + to_low * s, b[1] + to_high * s)


def factor_tree(element):
    factors = []
    for step in (1, 2, 4):
        factor, element = join_factor(element, [rolled(x, -step) for x in element])
        factors.append(factor)
    return factors, element


def source_tree(factors, source):
    offsets = []
    for step, factor in zip((1, 2, 4), factors):
        offset, source = join_source(factor, source, [rolled(x, -step) for x in source])
        offsets.append(offset)
    return offsets, source


def solve_tree(factors, offsets, low, high):
    row = sublane()
    for step, (to_low, to_high, *_), offset in reversed(list(zip((1, 2, 4), factors, offsets))):
        middle = offset + to_low * low + to_high * high
        upper = (row & step) != 0
        low, high = jnp.where(upper, rolled(middle, step), low), jnp.where(
            upper, rolled(high, step), middle
        )
    return low, high


def solve_chunk(factors, offsets, low, high):
    h = {-1: low, DEPTH - 1: high}
    for (m, lo, hi), (to_low, to_high, *_), offset in reversed(list(zip(ORDER, factors, offsets))):
        h[m] = offset + to_low * h[lo] + to_high * h[hi]
    return [h[k] for k in range(DEPTH)]


def gates(joints_ref):
    joints = joints_ref[...]
    flags = jnp.ones((1, SIDE), jnp.int32)
    for q in range(joints_ref.shape[0]):
        joint = joints[q : q + 1, :]
        at_edge = (joint & (SIDE - 1)) == 0
        device = lax.shift_right_logical(joint, SIDE.bit_length() - 1) & (DEVICES - 1)
        flags = flags | jnp.where(at_edge, jnp.left_shift(1, device), 0)
    row = lax.broadcasted_iota(jnp.int32, (DEVICES, SIDE), 0)
    flags = jnp.broadcast_to(flags, (DEVICES, SIDE))
    return jnp.where((lax.shift_right_logical(flags, row) & 1) != 0, 0.0, 1.0)


def outer_ends(gathered_ref, gates_ref, table_ref, ring_ref, me, turn):
    for d in range(DEVICES):
        member = lax.rem(me + (1 + d - turn) % DEVICES, DEVICES)
        for p in range(SLABS):
            at = d * ROWS + p * SLAB
            ring_ref[at : at + SLAB, :] = gathered_ref[SLABS * member + p]
        device = lax.rem(me + 1 + d, DEVICES)
        ring_ref[d * ROWS + OPEN : d * ROWS + OPEN + 1, :] = gates_ref[pl.ds(device, 1), :]
    own = sublane() == CHUNKS - 1

    def part(row, odd):
        return ring_ref[pl.ds(odd * ROWS + row, 8, stride=2 * ROWS), :]

    kinds_low, kinds_high = (
        [part(row, odd).astype(jnp.int32) for odd in range(2)] for row in (KIND_LOW, KIND_HIGH)
    )
    ends = []
    for c in range(2):
        values = [
            jnp.broadcast_to(table_ref[MATERIALS * c + q : MATERIALS * c + q + 1, :], own.shape)
            for q in range(MATERIALS)
        ]
        cells_low, cells_high = (
            [chosen(kind, values) for kind in kinds] for kinds in (kinds_low, kinds_high)
        )
        elements, sources = [], []
        for odd in range(2):
            before = cells_high[0] if odd else rolled(cells_high[1], 1)
            entry = (before + cells_low[odd]) * part(OPEN, odd)
            zero = jnp.zeros_like(entry)
            factor, element = join_factor(
                (zero, zero, entry), [part(2 * q + c, odd) for q in (G_LOW, G_HIGH, LINK)]
            )
            _, source = join_source(
                factor, (zero, zero), [part(2 * q + c, odd) for q in (S_LOW, S_HIGH)]
            )
            if odd:
                element = [
                    jnp.where(own, y, x) for x, y in zip(element, (zero, zero, entry))
                ]
                source = [jnp.where(own, 0.0, x) for x in source]
            elements.append(element)
            sources.append(source)
        factor, element = join_factor(*elements)
        _, source = join_source(factor, *sources)
        factors, element = factor_tree(element)
        _, source = source_tree(factors, source)

        def mine(q):
            at = (DEVICES - 1) * ROWS + 2 * q + c
            return ring_ref[at : at + 1, :]

        g_low = mine(G_LOW) + element[1][0:1, :]
        g_high = mine(G_HIGH) + element[0][0:1, :]
        link = mine(LINK) + element[2][0:1, :]
        s_low = mine(S_LOW) + source[1][0:1, :]
        s_high = mine(S_HIGH) + source[0][0:1, :]
        inverse = 1.0 / (g_low * g_high + link * (g_low + g_high))
        low = (s_low * (g_high + link) + link * s_high) * inverse
        high = (s_high * (g_low + link) + link * s_low) * inverse
        ends.append(
            (jnp.broadcast_to(low, (CHUNKS, SIDE)), jnp.broadcast_to(high, (CHUNKS, SIDE)))
        )
    return ends


def save(ref, c, at, values):
    for i, x in enumerate(values):
        ref[c, at + i] = x


CELLS = len(ORDER)
JOINS = CELLS + 3


def load_factors(ref, c):
    per = ref.shape[1] // JOINS
    factors = [tuple(ref[c, per * i + j] for j in range(per)) for i in range(JOINS)]
    return factors[:CELLS], factors[CELLS:]


def flatten(factors):
    return [x for factor in factors for x in factor]


def put(pay_ref, row, x):
    pay_ref[row : row + 1, :] = x


def static_rows(pay_ref, c, element):
    for q, x in zip((G_LOW, G_HIGH, LINK), element):
        put(pay_ref, 2 * q + c, x[0:1, :])


def kind_rows(pay_ref, kind_ref):
    for row, at in ((KIND_LOW, 0), (KIND_HIGH, SIDE - 1)):
        put(pay_ref, row, kind_ref[at : at + 1, :].astype(jnp.float32))


def source_rows(pay_ref, c, source):
    for q, x in zip((S_LOW, S_HIGH), source):
        put(pay_ref, 2 * q + c, x[0:1, :])


def spread(pay_ref, out_ref):
    for p in range(SLABS):
        slab = pay_ref[p * SLAB : (p + 1) * SLAB, :]
        for d in range(DEVICES):
            out_ref[SLABS * d + p] = slab


def reduce_kernel(
    fields_in, material_in, conduct_in, joints_x_in, joints_y_in,
    out_ref, x_factor_ref, x_offset_ref, y_factor_ref, y_pay_ref,
    x_gates_ref, y_gates_ref, table_ref,
    fields_ref, material_ref, conduct_ref, joints_x_ref, joints_y_ref,
    turned_ref, kind_ref, pay_ref, sems,
):
    at_x, at_y = lax.axis_index("gx"), lax.axis_index("gy")
    copies = [
        pltpu.make_async_copy(source, target, sems.at[i])
        for i, (source, target) in enumerate(
            (
                (joints_x_in, joints_x_ref),
                (joints_y_in, joints_y_ref),
                (conduct_in, conduct_ref),
                (material_in, material_ref),
                (fields_in, fields_ref),
            )
        )
    ]
    for copy in copies:
        copy.start()
    for copy in copies[:3]:
        copy.wait()
    flags_x, flags_y = (
        cut_bits(ref, at * SIDE) for ref, at in ((joints_x_ref, at_x), (joints_y_ref, at_y))
    )
    x_gates_ref[...] = gates(joints_x_ref)
    y_gates_ref[...] = gates(joints_y_ref)
    for c in range(2):
        for q in range(MATERIALS):
            table_ref[MATERIALS * c + q : MATERIALS * c + q + 1, :] = jnp.full(
                (1, SIDE), conduct_ref[c, q] * HALF_SCALE[c], jnp.float32
            )
    y_pay_ref[...] = jnp.zeros_like(y_pay_ref)
    copies[3].wait()
    kind_ref[...] = material_ref[...].T
    kind_rows(y_pay_ref, material_ref)
    cells = conductivities(lambda k: material_ref[pl.ds(k, CHUNKS, stride=DEPTH), :], conduct_ref)
    for c in range(2):
        factors, element = factor_chunk(face_links(cells[c], flags_y))
        tree, element = factor_tree(element)
        save(y_factor_ref, c, 0, flatten(factors + tree))
        static_rows(y_pay_ref, c, element)
    kind_rows(pay_ref, kind_ref)
    cells = conductivities(lambda k: kind_ref[pl.ds(k, CHUNKS, stride=DEPTH), :], conduct_ref)
    chunks = [factor_chunk(face_links(cells[c], flags_x)) for c in range(2)]
    trees = [factor_tree(element) for _, element in chunks]
    for c in range(2):
        static_rows(pay_ref, c, trees[c][1])
        save(x_factor_ref, c, 0, flatten(f[:2] for f in chunks[c][0] + trees[c][0]))
    copies[4].wait()
    for c in range(2):
        turned_ref[c] = fields_ref[c].T
    for c in range(2):
        sources = [turned_ref[c, pl.ds(k, CHUNKS, stride=DEPTH), :] for k in range(DEPTH)]
        offsets, source = source_chunk(chunks[c][0], sources)
        tree_offsets, source = source_tree(trees[c][0], source)
        save(x_offset_ref, c, 0, offsets + tree_offsets)
        source_rows(pay_ref, c, source)
    spread(pay_ref, out_ref)


def turn_kernel(
    gathered_ref, gates_ref, table_ref, x_factor_ref, x_offset_ref, y_factor_ref, y_pay_ref,
    half_ref, out_ref, y_offset_ref,
    ring_ref, turned_ref, pay_ref,
):
    ends = outer_ends(
        gathered_ref, gates_ref, table_ref, ring_ref, lax.axis_index("gx"), TURN_X
    )
    pay_ref[...] = y_pay_ref[...]
    for c in range(2):
        factors, tree = load_factors(x_factor_ref, c)
        offsets = [x_offset_ref[c, i] for i in range(JOINS)]
        low, high = solve_tree(tree, offsets[CELLS:], *ends[c])
        for k, h in enumerate(solve_chunk(factors, offsets[:CELLS], low, high)):
            turned_ref[c, pl.ds(k, CHUNKS, stride=DEPTH), :] = h
        half_ref[c] = turned_ref[c].T
    for c in range(2):
        factors, tree = load_factors(y_factor_ref, c)
        sources = [half_ref[c, pl.ds(k, CHUNKS, stride=DEPTH), :] for k in range(DEPTH)]
        offsets, source = source_chunk(factors, sources)
        tree_offsets, source = source_tree(tree, source)
        save(y_offset_ref, c, 0, offsets + tree_offsets)
        source_rows(pay_ref, c, source)
    spread(pay_ref, out_ref)


def finish_kernel(
    gathered_ref, gates_ref, table_ref, y_factor_ref, y_offset_ref, half_ref,
    half_out, advanced_out,
    ring_ref, advanced_ref, sems,
):
    copies = [pltpu.make_async_copy(half_ref, half_out, sems.at[2])]
    copies[0].start()
    ends = outer_ends(
        gathered_ref, gates_ref, table_ref, ring_ref, lax.axis_index("gy"), TURN_Y
    )
    for c in range(2):
        factors, tree = load_factors(y_factor_ref, c)
        offsets = [y_offset_ref[c, i] for i in range(JOINS)]
        low, high = solve_tree(tree, offsets[CELLS:], *ends[c])
        for k, h in enumerate(solve_chunk(factors, offsets[:CELLS], low, high)):
            advanced_ref[c, pl.ds(k, CHUNKS, stride=DEPTH), :] = h
        copies.append(pltpu.make_async_copy(advanced_ref.at[c], advanced_out.at[c], sems.at[c]))
        copies[-1].start()
    for copy in copies:
        copy.wait()


TURN_X = 11
TURN_Y = 10


def turned_exchange(x, axis, turn):
    group = [(i + turn) % DEVICES for i in range(DEVICES)]
    return lax.all_to_all(x, axis, 0, 0, axis_index_groups=[group], tiled=True)


def f32(*shape):
    return jax.ShapeDtypeStruct(shape, jnp.float32)


VMEM = pl.BlockSpec(memory_space=pltpu.VMEM)
HBM = pl.BlockSpec(memory_space=pltpu.HBM)
SPREAD = (DEVICES * SLABS, SLAB, SIDE)
PARAMS = pltpu.CompilerParams(vmem_limit_bytes=8 << 20)
BLOCK = (2, SIDE, SIDE)
FACTORS_X = (2, 2 * JOINS, CHUNKS, SIDE)
FACTORS_Y = (2, 3 * JOINS, CHUNKS, SIDE)
OFFSET = (2, JOINS, CHUNKS, SIDE)


def per_device(fields, material, conduct, joints_x, joints_y):
    inputs = (fields, material, conduct, joints_x.T, joints_y.T)
    with jax.named_scope("reduce_x"):
        pay, x_factor, x_offset, y_factor, y_pay, x_gates, y_gates, table = pl.pallas_call(
            reduce_kernel,
            out_shape=(f32(*SPREAD), f32(*FACTORS_X), f32(*OFFSET), f32(*FACTORS_Y))
            + (f32(ROWS, SIDE), f32(DEVICES, SIDE), f32(DEVICES, SIDE), f32(2 * MATERIALS, SIDE)),
            in_specs=[HBM] * 5,
            out_specs=(VMEM,) * 8,
            scratch_shapes=[
                pltpu.VMEM(BLOCK, jnp.float32),
                pltpu.VMEM((SIDE, SIDE), jnp.int32),
                pltpu.SMEM(conduct.shape, jnp.float32),
                pltpu.VMEM(joints_x.shape[::-1], jnp.int32),
                pltpu.VMEM(joints_y.shape[::-1], jnp.int32),
                pltpu.VMEM(BLOCK, jnp.float32),
                pltpu.VMEM((SIDE, SIDE), jnp.int32),
                pltpu.VMEM((ROWS, SIDE), jnp.float32),
                pltpu.SemaphoreType.DMA((5,)),
            ],
            compiler_params=PARAMS,
        )(*(pltpu.with_memory_space_constraint(x, pltpu.HBM) for x in inputs))
    with jax.named_scope("exchange_x"):
        gathered = turned_exchange(pay, "gx", TURN_X)
    with jax.named_scope("solve_x_reduce_y"):
        half, pay, y_offset = pl.pallas_call(
            turn_kernel,
            out_shape=(f32(*BLOCK), f32(*SPREAD), f32(*OFFSET)),
            in_specs=[VMEM] * 7,
            out_specs=(VMEM,) * 3,
            scratch_shapes=[
                pltpu.VMEM((DEVICES * ROWS, SIDE), jnp.float32),
                pltpu.VMEM(BLOCK, jnp.float32),
                pltpu.VMEM((ROWS, SIDE), jnp.float32),
            ],
            compiler_params=PARAMS,
        )(gathered, x_gates, table, x_factor, x_offset, y_factor, y_pay)
    with jax.named_scope("exchange_y"):
        gathered = turned_exchange(pay, "gy", TURN_Y)
    with jax.named_scope("solve_y"):
        return pl.pallas_call(
            finish_kernel,
            out_shape=(f32(*BLOCK), f32(*BLOCK)),
            in_specs=[VMEM] * 6,
            out_specs=(HBM, HBM),
            scratch_shapes=[
                pltpu.VMEM((DEVICES * ROWS, SIDE), jnp.float32),
                pltpu.VMEM(BLOCK, jnp.float32),
                pltpu.SemaphoreType.DMA((3,)),
            ],
            compiler_params=PARAMS,
        )(gathered, y_gates, table, y_factor, y_offset, half)


def solution(mesh):
    return jax.shard_map(
        per_device,
        mesh=mesh,
        in_specs=(P(None, "gy", "gx"), P("gy", "gx"), P(), P("gy", None), P("gx", None)),
        out_specs=(P(None, "gy", "gx"), P(None, "gy", "gx")),
        check_vma=False,
    )
```
